32 devices in a mesh: grp: 4 (over y, x), seq: 8 (over z, core).
Axes of the slice: x: 2, y: 2, z: 4, core: 2. Of those that a mesh axis runs over, the one named last changes fastest.
Arguments:
- queries: bfloat16 [4096, 1024], P(('grp', 'seq')), may hold values from -6 to 6
- keys: bfloat16 [4096, 1024], P(('grp', 'seq')), may hold values from -11 to 11
- values: bfloat16 [4096, 1024], P(('grp', 'seq')), may hold values from -6 to 6
- forget: float32 [4096, 8], P(('grp', 'seq')), may hold values from 0 to 0.5
- beta: float32 [4096, 8], P(('grp', 'seq')), may hold values from 0 to 1
- level_weights: float32 [9, 4096, 8], P(None, ('grp', 'seq')), may hold values from 0.25 to 2
Outputs:
- output: float32 [4096, 1024], P(('grp', 'seq'))
The draws below stay inside these ranges and needn't reach their ends.
All inputs are finite; a program needn't handle non-finite values.
Results may differ from the reference program's by a relative error of at most 0.0003.
Values sent between devices are 32-bit elements; how exact they have to be, the bound alone decides.
A program may use at most 64 MiB of HBM per device.

```python
import math
import jax
import jax.numpy as jnp
from jax import lax

HEADS = 8
HEAD_DIM = 128
BLOCK = 128
LEVELS = 8
TOK_DEV = 128
TOKENS = 4096
N_GRP = 4
N_SEQ = 8


def slow_heads(key):
    order = jax.random.permutation(jax.random.fold_in(key, 11), HEADS)
    count = HEADS // 2
    return order < count


def device_factor(key, salt):
    factor = jax.random.uniform(jax.random.fold_in(key, salt), (TOKENS // TOK_DEV, HEADS), jnp.float32, 0.6, 1.6)
    return jnp.repeat(factor, TOK_DEV, axis=0)


def draw_keys(key, part):
    subkeys = jax.random.split(jax.random.fold_in(key, 41), 3)
    noise_part = jnp.clip(jax.random.normal(subkeys[0], (TOKENS, HEADS, HEAD_DIM), jnp.float32), -6.0, 6.0)
    sign_pattern = (jax.random.randint(subkeys[1], (HEADS, HEAD_DIM), 0, 2) * 2 - 1).astype(jnp.float32)
    shared_scale = jax.random.uniform(subkeys[2], (TOKENS, HEADS), jnp.float32, 2.4, 3.6)
    result = noise_part + shared_scale[:, :, None] * sign_pattern[None, :, :]
    return result.reshape(TOKENS, HEADS * HEAD_DIM).astype(jnp.bfloat16)


def draw_forget(key, part):
    slow = slow_heads(key)
    subkeys = jax.random.split(jax.random.fold_in(key, 21), 6)
    slow_rate = jax.random.uniform(subkeys[0], (HEADS,), jnp.float32, 0.1, 0.5) / TOKENS
    fast_rate = jax.random.uniform(subkeys[1], (HEADS,), jnp.float32, 1.0 / 500.0, 1.0 / 250.0)
    base_rate = jnp.where(slow, slow_rate, fast_rate)
    rough = jax.random.uniform(subkeys[2], (TOKENS, HEADS), jnp.float32, 0.5, 1.5)
    result = base_rate[None, :] * device_factor(key, 23) * rough
    first_spot = jax.random.randint(subkeys[3], (HEADS,), 0, TOKENS)
    offset = jax.random.randint(subkeys[5], (HEADS,), 1, TOKENS)
    second_spot = (first_spot + offset) % TOKENS
    spots = jnp.stack([first_spot, second_spot], 0)
    amount = jax.random.uniform(subkeys[4], (2, HEADS), jnp.float32, 0.22, 0.4)
    columns = jnp.broadcast_to(jnp.arange(HEADS)[None, :], (2, HEADS))
    return result.at[spots, columns].add(amount)


def draw_beta(key, part):
    slow = slow_heads(key)
    subkeys = jax.random.split(jax.random.fold_in(key, 31), 3)
    slow_base = jax.random.uniform(subkeys[0], (HEADS,), jnp.float32, 0.5, 1.5) * 3.0 * HEAD_DIM / TOKENS
    fast_base = jax.random.uniform(subkeys[1], (HEADS,), jnp.float32, 0.2, 0.7)
    base_value = jnp.where(slow, slow_base, fast_base)
    rough = jax.random.uniform(subkeys[2], (TOKENS, HEADS), jnp.float32, 0.7, 1.3)
    return base_value[None, :] * rough


def block_scale(own_key, dims, shards, least, high):
    def one(dim, blocks):
        heights = jax.random.uniform(jax.random.fold_in(jax.random.fold_in(own_key, 6), dim), (blocks,), jnp.float32, least / len(shards), high / len(shards))
        return jnp.repeat(jnp.exp(heights), dims[dim] // blocks).reshape((-1,) + (1,) * (len(dims) - dim - 1))

    factor_of = one(*shards[0])
    for cut in shards[1:]:
        factor_of = factor_of * one(*cut)
    return factor_of


def centred(key, shape, spread, reach, cuts=(), held_as=jnp.bfloat16):
    gain = block_scale(key, shape, cuts, -0.22, 0.18) if cuts else 1.0
    values = jax.random.normal(key, shape, jnp.float32) * spread * gain
    return jnp.minimum(jnp.maximum(values, -reach), reach).astype(held_as)


def setup_inputs(seed: int = 0) -> dict:
    splits = jax.random.split(jax.random.key(seed), 7)
    queries = centred(splits[0], (TOKENS, HEADS * HEAD_DIM), 1.0, 6.0, ((0, 32),))
    keys = draw_keys(jax.random.fold_in(splits[6], 71), 0)
    values = centred(splits[2], (TOKENS, HEADS * HEAD_DIM), 1.0, 6.0, ((0, 32),))
    forget = draw_forget(jax.random.fold_in(splits[6], 71), 0)
    beta = draw_beta(jax.random.fold_in(splits[6], 71), 0)
    level_weights = jnp.clip(jnp.exp(math.log(2.0) - 2.0794415 * jax.random.uniform(splits[5], (LEVELS + 1, TOKENS, HEADS), jnp.float32) ** block_scale(splits[5], (LEVELS + 1, TOKENS, HEADS), ((1, 32),), -0.2, 0.2)), 0.25, 2.0)
    return {"queries": queries, "keys": keys, "values": values, "forget": forget, "beta": beta, "level_weights": level_weights}


def contract(form, left, right):
    return jnp.einsum(form, left, right, precision=lax.Precision.HIGHEST)

def unit_rows(array):
    return array * lax.rsqrt(lax.optimization_barrier(jnp.sum(array * array, -1, keepdims=True)) + 1e-06)

def block_step(carry, pieces):
    memory, transition = carry
    query_block, key_block, value_block, forget_block, beta_block = pieces
    length = query_block.shape[0]
    head_dim = query_block.shape[-1]
    query_heads = unit_rows(jnp.swapaxes(query_block.astype(jnp.float32), 0, 1))
    key_heads = unit_rows(jnp.swapaxes(key_block.astype(jnp.float32), 0, 1))
    value_heads = jnp.swapaxes(value_block.astype(jnp.float32), 0, 1)
    decays = jnp.exp(-jnp.cumsum(forget_block, 0)).T
    strength = beta_block.T
    strict = jnp.tril(jnp.ones((length, length), jnp.float32), -1)
    causal = jnp.tril(jnp.ones((length, length), jnp.float32), 0)
    intersections = contract('hsk,htk->hst', key_heads, key_heads)
    unit_lower = jnp.eye(length, dtype=jnp.float32) + strength[:, :, None] * intersections * strict
    right_sides = jnp.concatenate([strength[:, :, None] * key_heads, (strength / decays)[:, :, None] * value_heads], -1)
    solved = lax.linalg.triangular_solve(unit_lower, right_sides, left_side=True, lower=True, unit_diagonal=True)
    update_rows = solved[..., :head_dim]
    write_rows = solved[..., head_dim:]
    scores = contract('htk,hsk->hts', query_heads, key_heads) * causal
    reached = decays[:, :, None] * (query_heads - contract('hts,hsk->htk', scores, update_rows))
    inside = decays[:, :, None] * contract('hts,hsv->htv', scores, write_rows) + contract('hvk,htk->htv', memory, reached)
    reach_dev = contract('hkj,htj->htk', transition, reached)
    final_decay = decays[:, -1][:, None, None]
    step_trans = final_decay * (jnp.eye(head_dim, dtype=jnp.float32) - contract('hsk,hsj->hkj', update_rows, key_heads))
    step_write = final_decay * contract('hsv,hsk->hvk', write_rows, key_heads)
    memory = contract('hvk,hkj->hvj', memory, step_trans) + step_write
    transition = contract('hik,hkj->hij', transition, step_trans)
    return ((memory, transition), (inside, reach_dev))

def reference(queries, keys, values, forget, beta, level_weights):
    devices = N_GRP * N_SEQ
    blocks = TOK_DEV // BLOCK

    def per_device(array):
        return array.reshape((devices, blocks, BLOCK) + array.shape[1:])
    shaped = (TOKENS, HEADS, HEAD_DIM)
    weights_dev = jnp.transpose(level_weights, (1, 0, 2)).reshape(devices, TOK_DEV, LEVELS + 1, HEADS)
    items = (per_device(queries.reshape(shaped)), per_device(keys.reshape(shaped)), per_device(values.reshape(shaped)), per_device(forget), per_device(beta), weights_dev, jnp.arange(devices, dtype=jnp.int32))
    spans = jnp.left_shift(jnp.int32(1), jnp.arange(LEVELS, dtype=jnp.int32))

    def device_step(levels, entry):
        query_dev, key_dev, value_dev, forget_dev, beta_dev, weight_dev, number = entry
        start = (jnp.zeros((HEADS, HEAD_DIM, HEAD_DIM), jnp.float32), jnp.broadcast_to(jnp.eye(HEAD_DIM, dtype=jnp.float32), (HEADS, HEAD_DIM, HEAD_DIM)))
        (memory, transition), (inside, reached) = lax.scan(block_step, start, (query_dev, key_dev, value_dev, forget_dev, beta_dev))
        inside = jnp.swapaxes(inside, 0, 1).reshape(HEADS, TOK_DEV, HEAD_DIM)
        reached = jnp.swapaxes(reached, 0, 1).reshape(HEADS, TOK_DEV, HEAD_DIM)
        weighted = jnp.transpose(weight_dev[:, 1:, :], (1, 2, 0))[:, :, :, None] * reached[None]
        far_part = contract('lhtk,lhvk->htv', weighted, levels)
        result = weight_dev[:, 0, :].T[:, :, None] * inside + far_part
        following = number + 1
        below = following % (2 * spans) == 0
        target = jnp.logical_and(following % spans == 0, jnp.logical_not(below))
        moved = contract('lhvk,hkj->lhvj', levels, transition)
        merged = contract('lhvk,hkj->hvj', levels * below.astype(jnp.float32)[:, None, None, None], transition) + memory
        cleared = jnp.logical_or(below, target)[:, None, None, None]
        levels = jnp.where(cleared, jnp.zeros_like(moved), moved) + target.astype(jnp.float32)[:, None, None, None] * merged[None]
        return (levels, result)
    zeros = jnp.zeros((LEVELS, HEADS, HEAD_DIM, HEAD_DIM), jnp.float32)
    unused, results = lax.scan(device_step, zeros, items)
    return jnp.transpose(results, (0, 2, 1, 3)).reshape(TOKENS, HEADS * HEAD_DIM)
```

```python
import functools

import jax
import jax.numpy as jnp
from jax import lax
from jax.experimental import pallas as pl
from jax.experimental.pallas import tpu as pltpu
from jax.sharding import PartitionSpec as P

MESH = pl.DeviceIdType.MESH
F32 = jnp.float32
BF16 = jnp.bfloat16
NN = (((1,), (0,)), ((), ()))
NT = (((1,), (1,)), ((), ()))
AUX = 16
TILE = 16
EPS = 1e-06


def dot(a, b, dims=NN):
    return lax.dot_general(a, b, dims, preferred_element_type=F32)


def split(a):
    high = a.astype(BF16)
    return high, (a - high.astype(F32)).astype(BF16)


def mm(a, b):
    ah, al = a
    bh, bl = b
    return dot(ah, bh) + (dot(ah, bl) + dot(al, bh))


def mm_square(a, b):
    ah, al = a
    bh, bl = b
    right = jnp.concatenate(
        [jnp.concatenate([bh, bl], 1), jnp.concatenate([bh, jnp.zeros_like(bl)], 1)], 0
    )
    both = dot(jnp.concatenate([ah, al], 1), right)
    width = bh.shape[1]
    return both[:, :width] + both[:, width:]


def mm_exact(a, b):
    return dot(jnp.concatenate(a, 1), jnp.concatenate([b, b], 0))


def tile_inverse(low, size):
    lane = lax.broadcasted_iota(jnp.int32, (TILE, size), 1)
    sub = lax.broadcasted_iota(jnp.int32, (TILE, size), 0)
    tile = lane // TILE
    packed = low[:TILE]
    for g in range(1, size // TILE):
        packed = jnp.where(tile == g, low[g * TILE : (g + 1) * TILE], packed)
    inner = lane - tile * TILE
    packed = jnp.where(sub > inner, packed, 0.0)
    x = jnp.where(sub == inner, 1.0, 0.0)
    for c in range(TILE - 1):
        column = jnp.take_along_axis(packed, tile * TILE + c, axis=1)
        x = x - column * x[c : c + 1]
    return jnp.concatenate(
        [jnp.where(tile == g, x, 0.0) for g in range(size // TILE)], 0
    )


def unit_lower_inverse(lowers, size, row, col):
    apart = row ^ col
    inverses = [tile_inverse(low, size) for low in lowers]
    width = TILE
    while width < size:
        mask = (apart >= width) & (apart < 2 * width)
        parts = [split(x) for x in inverses]
        blocks = [split(jnp.where(mask, low, 0.0)) for low in lowers]
        left = [split(mm_square(x, b)) for x, b in zip(parts, blocks)]
        inverses = [x - mm_square(l, p) for x, l, p in zip(inverses, left, parts)]
        width *= 2
    return inverses


def transitions(blocks, size, dim):
    row = lax.broadcasted_iota(jnp.int32, (size, size), 0)
    col = lax.broadcasted_iota(jnp.int32, (size, size), 1)
    aux_row = lax.broadcasted_iota(jnp.int32, (AUX, size), 0)
    staged, lowers = [], []
    for kb, vb, aux in blocks:
        gram = dot(kb, kb, NT)
        norm = jnp.sum(jnp.where(row == col, gram, 0.0), 0, keepdims=True) + EPS
        rk = lax.rsqrt(norm)
        gain = aux[1:2] * (rk * rk)
        decay = aux[0:1]
        cols = jnp.where(aux_row == AUX - 1, gain, aux).T
        lowers.append(jnp.where(row > col, gram * gain, 0.0))
        staged.append((kb, vb, gain, norm * rk / decay, decay[:, size - 1 : size], cols))
    inverses = unit_lower_inverse(lowers, size, row, col)
    eye = (row == col).astype(F32)
    results = []
    for inverse, (kb, vb, gain, unscale, last, cols) in zip(inverses, staged):
        y = mm_exact(split(inverse), kb)
        z = mm_exact(split(inverse * unscale), vb)
        pair = jnp.concatenate([y, z], 1)
        kt = kb.astype(F32).T.astype(BF16)
        moved = dot(
            jnp.concatenate([kt, kt], 1),
            jnp.concatenate(split(pair * cols[:, AUX - 1 : AUX]), 0),
        )
        node = jnp.concatenate([last * (eye - moved[:, :dim]), last * moved[:, dim:]], 1)
        results.append((node, pair, cols, gain))
    return results


def local_reads(qb, kb, pair, cols, gain):
    size = qb.shape[0]
    dim = qb.shape[1]
    row = lax.broadcasted_iota(jnp.int32, (size, size), 0)
    col = lax.broadcasted_iota(jnp.int32, (size, size), 1)
    q = qb.astype(F32)
    scale = lax.rsqrt(jnp.sum(q * q, -1, keepdims=True) + EPS) * cols[:, 0:1]
    scores = jnp.where(row >= col, dot(qb, kb, NT) * gain, 0.0)
    seen = mm(split(scores), split(pair))
    return scale * (q - seen[:, :dim]), (scale * cols[:, 2:3]) * seen[:, dim:]


def join(lower, upper, dim):
    both = mm(split(upper[:, :dim]), split(lower))
    return jnp.concatenate([both[:, :dim], both[:, dim:] + upper[:, dim:]], 1)


def kernel(n_grp, n_seq, heads, *refs):
    q_ref, k_ref, v_ref, f_ref, b_ref, w_ref, out_ref = refs[:7]
    (
        aux,
        kv_out,
        q_out,
        kv_in,
        q_in,
        pairs,
        colb,
        gains,
        blocks,
        nodes,
        node_in,
        r_out,
        r_in,
        colr,
        near,
        near_in,
        far,
        far_in,
        joined,
    ) = refs[7:26]
    refs = refs[26:]
    total_bits = (n_grp * n_seq).bit_length() - 1
    cross = n_seq.bit_length() - 1
    middle = list(range(2, cross))
    upward = list(range(cross + 1, total_bits))
    n_mid, n_up = len(middle), len(upward)
    mids, refs = refs[:n_mid], refs[n_mid:]
    up_out, up_in, refs = refs[:n_up], refs[n_up : 2 * n_up], refs[2 * n_up :]
    (
        s_kv,
        r_kv,
        s_q,
        r_q,
        s_node,
        r_node,
        s_r,
        r_r,
        s_mid,
        r_mid,
        s_up,
        r_up,
        s_near,
        r_near,
        s_far,
        r_far,
    ) = refs
    size = q_ref.shape[0]
    dim = q_ref.shape[1] // heads
    slots = heads // 2
    pos = lax.axis_index("grp") * n_seq + lax.axis_index("seq")

    def bit_of(l):
        return (pos // (1 << l)) % 2

    core, zl, xx = bit_of(0), bit_of(1), bit_of(cross)
    base = pos - core - 2 * zl - xx * (1 << cross)
    place = 2 * xx + zl

    def where_is(number):
        return (number // n_seq, number % n_seq)

    def place_of(m):
        return 2 * (1 - xx if m & 2 else xx) + (1 - zl if m & 1 else zl)

    def member(m, c):
        z = 1 - zl if m & 1 else zl
        x = 1 - xx if m & 2 else xx
        return where_is(base + c + 2 * z + x * (1 << cross))

    def partner(l):
        return where_is(pos + (1 - 2 * bit_of(l)) * (1 << l))

    def columns(i):
        return pl.ds(pl.multiple_of(i * dim, dim), dim)

    def remote(source, target, send, receive, device):
        return pltpu.make_async_remote_copy(
            src_ref=source,
            dst_ref=target,
            send_sem=send,
            recv_sem=receive,
            device_id=device,
            device_id_type=MESH,
        )

    other = 1 - core
    barrier = pltpu.get_barrier_semaphore()
    for m in range(4):
        for c in (core, other):
            if m or c is other:
                pl.semaphore_signal(barrier, inc=1, device_id=member(m, c), device_id_type=MESH)
    for l in middle + upward:
        pl.semaphore_signal(barrier, inc=1, device_id=partner(l), device_id_type=MESH)

    total = f_ref[...]
    lane = lax.broadcasted_iota(jnp.int32, total.shape, 1)
    step = 1
    while step < size:
        total = total + jnp.where(lane >= step, pltpu.roll(total, step, 1), 0.0)
        step *= 2
    decay = jnp.exp(-total)
    aux[...] = jnp.zeros_like(aux)
    levels = w_ref.shape[0]
    for h in range(heads):
        aux[h, 0:1] = decay[h : h + 1]
        aux[h, 1:2] = b_ref[h : h + 1]
        for l in range(levels):
            aux[h, 2 + l : 3 + l] = w_ref[l, h : h + 1]

    order = (0, 3, 1, 2)
    for j in order:
        h = other * slots + j
        kv_out[j, :size] = k_ref[:, columns(h)].astype(F32)
        kv_out[j, size : 2 * size] = v_ref[:, columns(h)].astype(F32)
        kv_out[j, 2 * size :] = aux[h]
        q_out[j] = q_ref[:, columns(h)].astype(F32)
    pl.semaphore_wait(barrier, 7 + n_mid + n_up)

    pending = []
    kv_copies, q_copies = {}, {}
    for j in order:
        kv_copies[j] = remote(
            kv_out.at[j], kv_in.at[j], s_kv.at[j], r_kv.at[j], member(0, other)
        )
        q_copies[j] = remote(q_out.at[j], q_in.at[j], s_q.at[j], r_q.at[j], member(0, other))
    for copies in (kv_copies, q_copies):
        for j in order:
            copies[j].start()
            pending.append(copies[j])

    def own_block(j):
        h = core * slots + j
        return k_ref[:, columns(h)], v_ref[:, columns(h)], aux[h]

    def other_block(j):
        return (
            kv_in[j, :size].astype(BF16),
            kv_in[j, size : 2 * size].astype(BF16),
            kv_in[j, 2 * size :],
        )

    def solve(work):
        done = transitions(
            [own_block(j) if e == 0 else other_block(j) for j, e in work], size, dim
        )
        for (j, e), (node, pair, cols, gain) in zip(work, done):
            blocks[other if e else core, j] = node
            pairs[e, j] = pair
            colb[e, j] = cols
            gains[e, j] = jnp.broadcast_to(gain, (8, size))

    node_copies, r_copies = {}, {}
    for m in range(1, 4):
        node_copies[m] = remote(
            nodes.at[place_of(m)],
            node_in.at[place],
            s_node.at[m],
            r_node.at[m],
            member(m, core),
        )
        r_copies[m] = [
            remote(
                r_out.at[place_of(m), s],
                r_in.at[place, s],
                s_r.at[2 * m + s],
                r_r.at[2 * m + s],
                member(m, core),
            )
            for s in range(2)
        ]
        pending.append(node_copies[m])
        pending += r_copies[m]

    def send_group(group, start):
        diagonal = (zl == xx) if group == 0 else (zl != xx)
        straight = (zl != xx) if group == 0 else (zl == xx)

        @pl.when(diagonal)
        def _():
            start(3)

        @pl.when(straight)
        def _():
            start(1)
            start(2)

    def merge(group):
        for j in group:
            nodes[j] = join(blocks[0, j], blocks[1, j], dim)

    def send_nodes(m):
        node_copies[m].start()

    def send_reads(m):
        for copy in r_copies[m]:
            copy.start()

    groups = ((0, 3), (1, 2))
    solve([(j, 0) for j in groups[0]])
    for j in groups[0]:
        kv_copies[j].wait_recv()
    solve([(j, 1) for j in groups[0]] + [(j, 0) for j in groups[1]])
    merge(groups[0])
    send_group(0, send_nodes)
    for j in groups[1]:
        kv_copies[j].wait_recv()
    solve([(j, 1) for j in groups[1]])
    merge(groups[1])
    send_group(1, send_nodes)

    def reads(group):
        for j in group:
            q_copies[j].wait_recv()
        for j in group:
            h = core * slots + j
            for e in range(2):
                if e == 0:
                    qb, kb, _ = q_ref[:, columns(h)], k_ref[:, columns(h)], None
                else:
                    qb, kb = q_in[j].astype(BF16), kv_in[j, :size].astype(BF16)
                s = other if e else core
                r, inside = local_reads(qb, kb, pairs[e, j], colb[e, j], gains[e, j, :1])
                r_out[j, s, :size] = r
                r_out[j, s, size:] = kv_in[j, 2 * size :] if e else aux[h]
                near[j, s] = inside
        for j in group:
            seen = mm(split(r_out[j, 1, :size]), split(blocks[0, j]))
            weight = jnp.where(core == 1, colb[0, j], colb[1, j])[:, 3:4]
            r_out[j, 1, :size] = seen[:, :dim]
            near[j, 1] += weight * seen[:, dim:]

    reads(groups[0])

    node_in[place] = nodes[place]
    for m in range(1, 4):
        node_copies[m].wait_recv()

    def send_mid(m, x):
        mine = bit_of(middle[m])
        copy = remote(
            mids[m].at[x, mine],
            mids[m].at[x, mine],
            s_mid.at[m, x],
            r_mid.at[m, x],
            partner(middle[m]),
        )
        copy.start()
        pending.append(copy)

    def wait_mid(m, x):
        theirs = 1 - bit_of(middle[m])
        remote(
            mids[m].at[x, theirs],
            mids[m].at[x, theirs],
            s_mid.at[m, x],
            r_mid.at[m, x],
            partner(middle[m]),
        ).wait_recv()

    for x in range(2):
        mids[0][x, bit_of(middle[0])] = join(node_in[2 * x], node_in[2 * x + 1], dim)
    for x in range(2):
        send_mid(0, x)

    send_group(0, send_reads)
    reads(groups[1])
    send_group(1, send_reads)
    near_copies = []
    for j in range(slots):
        copy = remote(
            near.at[j, other], near_in.at[j], s_near.at[j], r_near.at[j], member(0, other)
        )
        copy.start()
        near_copies.append(copy)
        pending.append(copy)
    for s in range(2):
        r_in[place, s] = r_out[place, s]

    for m in range(n_mid):
        for x in range(2):
            wait_mid(m, x)
        for x in range(2):
            node = join(mids[m][x, 0], mids[m][x, 1], dim)
            if m + 1 < n_mid:
                mids[m + 1][x, bit_of(middle[m + 1])] = node
            else:
                joined[x] = node
        if m + 1 < n_mid:
            for x in range(2):
                send_mid(m + 1, x)
    whole = join(joined[0], joined[1], dim)

    def send_up(m):
        copy = remote(up_out[m], up_in[m], s_up.at[m], r_up.at[m], partner(upward[m]))
        copy.start()
        pending.append(copy)
        return copy

    up_out[0][...] = whole[:, dim:] if n_up == 1 else whole
    copy = send_up(0)

    for m in range(1, 4):
        for c in r_copies[m]:
            c.wait_recv()
    for i in range(4):
        for s in range(2):
            colr[i, s] = r_in[i, s, size:].T

    def read(items, lower, l, gate=None, fresh=False):
        rows = jnp.concatenate([r_in[i, s, :size] for i, s in items], 0)
        seen = mm(split(rows), lower)
        for n, (i, s) in enumerate(items):
            part = seen[n * size : (n + 1) * size]
            value = colr[i, s][:, 3 + l : 4 + l] * part[:, part.shape[1] - dim :]
            if gate is not None:
                value = jnp.where(gate, value, 0.0)
            far[i, s] = value if fresh else far[i, s] + value
            if part.shape[1] > dim:
                new = part[:, :dim]
                r_in[i, s, :size] = (
                    new if gate is None else jnp.where(gate, new, r_in[i, s, :size])
                )

    for x in range(2):
        for s in range(2):
            far[2 * x, s] = jnp.zeros((size, dim), F32)
        read([(2 * x + 1, 0), (2 * x + 1, 1)], split(node_in[2 * x]), 1, fresh=True)
    for m, l in enumerate(middle):
        gate = bit_of(l) == 1
        for x in range(2):
            items = [(2 * x + z, s) for z in range(2) for s in range(2)]
            read(items, split(mids[m][x, 0]), l, gate)
    read([(2 + z, s) for z in range(2) for s in range(2)], split(joined[0]), cross)

    everyone = [(i, s) for i in range(4) for s in range(2)]
    for m, l in enumerate(upward):
        gate = bit_of(l) == 1
        copy.wait_recv()
        if m + 1 < n_up:
            peer, mine = up_in[m][...], up_out[m][...]
            node = join(jnp.where(gate, peer, mine), jnp.where(gate, mine, peer), dim)
            up_out[m + 1][...] = node[:, dim:] if m + 2 == n_up else node
            copy = send_up(m + 1)
            read(everyone, split(peer), l, gate)

    gate = bit_of(upward[-1]) == 1
    lower = split(up_in[-1][...])
    far_copies = {}
    for m in (3, 2, 1, 0):
        i = place_of(m)
        for e in (1, 0):
            s = other if e else core
            seen = mm(split(r_in[i, s, :size]), lower)
            weight = colr[i, s][:, 3 + upward[-1] : 4 + upward[-1]]
            far[i, s] += jnp.where(gate, weight * seen, 0.0)
            if m == 0 and e == 0:
                far_in[core * slots + place] = far[place, core]
                continue
            far_copies[m, e] = remote(
                far.at[i, s],
                far_in.at[core * slots + place],
                s_far.at[2 * m + e],
                r_far.at[2 * m + e],
                member(m, s),
            )
            far_copies[m, e].start()
            pending.append(far_copies[m, e])

    for copy in near_copies:
        copy.wait_recv()
    for m in range(4):
        for e in range(2):
            c = other if e else core
            j = place_of(m)
            h = c * slots + j
            if m or e:
                remote(
                    far.at[j, core],
                    far_in.at[h],
                    s_far.at[2 * m + e],
                    r_far.at[2 * m + e],
                    member(m, c),
                ).wait_recv()
            mine = near_in[j] if e else near[j, core]
            out_ref[:, columns(h)] = mine + far_in[h]
    for copy in pending:
        copy.wait_send()


def on_device(n_grp, n_seq, queries, keys, values, forget, beta, level_weights):
    size = queries.shape[0]
    heads = forget.shape[1]
    dim = queries.shape[1] // heads
    slots = heads // 2
    total_bits = (n_grp * n_seq).bit_length() - 1
    cross = n_seq.bit_length() - 1
    n_mid, n_up = cross - 2, total_bits - cross - 1
    node = (dim, 2 * dim)
    dma = pltpu.SemaphoreType.DMA

    def vmem(*shape):
        return pltpu.VMEM(shape, F32)

    ups = [vmem(*node)] * (n_up - 1) + [vmem(dim, dim)]
    return pl.pallas_call(
        functools.partial(kernel, n_grp, n_seq, heads),
        out_shape=pltpu.VMEM((size, heads * dim), F32),
        in_specs=[pl.BlockSpec(memory_space=pltpu.VMEM)] * 6,
        out_specs=pl.BlockSpec(memory_space=pltpu.VMEM),
        scratch_shapes=[
            vmem(heads, AUX, size),
            vmem(slots, 2 * size + AUX, dim),
            vmem(slots, size, dim),
            vmem(slots, 2 * size + AUX, dim),
            vmem(slots, size, dim),
            vmem(2, slots, size, 2 * dim),
            vmem(2, slots, size, AUX),
            vmem(2, slots, 8, size),
            vmem(2, slots, *node),
            vmem(slots, *node),
            vmem(4, *node),
            vmem(slots, 2, size + AUX, dim),
            vmem(4, 2, size + AUX, dim),
            vmem(4, 2, size, AUX),
            vmem(slots, 2, size, dim),
            vmem(slots, size, dim),
            vmem(4, 2, size, dim),
            vmem(heads, size, dim),
            vmem(2, *node),
        ]
        + [vmem(2, 2, *node)] * n_mid
        + ups
        + ups
        + [dma((slots,))] * 4
        + [dma((4,))] * 2
        + [dma((8,))] * 2
        + [dma((n_mid, 2))] * 2
        + [dma((n_up,))] * 2
        + [dma((slots,))] * 2
        + [dma((8,))] * 2,
        compiler_params=pltpu.CompilerParams(collective_id=0, has_side_effects=True),
    )(
        queries,
        keys,
        values,
        forget.T,
        beta.T,
        jnp.transpose(level_weights, (0, 2, 1)),
    )


def solution(mesh):
    both = P(("grp", "seq"), None)
    return jax.shard_map(
        functools.partial(on_device, mesh.shape["grp"], mesh.shape["seq"]),
        mesh=mesh,
        in_specs=(both, both, both, both, both, P(None, ("grp", "seq"), None)),
        out_specs=both,
        check_vma=False,
    )
```

```python
import functools

import jax
import jax.numpy as jnp
from jax import lax
from jax.experimental import pallas as pl
from jax.experimental.pallas import tpu as pltpu
from jax.sharding import PartitionSpec as P

MESH = pl.DeviceIdType.MESH
F32 = jnp.float32
BF16 = jnp.bfloat16
NN = (((1,), (0,)), ((), ()))
NT = (((1,), (1,)), ((), ()))
AUX = 16
ROWS = 8
TILE = 16
EPS = 1e-06


def dot(a, b, dims=NN):
    return lax.dot_general(a, b, dims, preferred_element_type=F32)


def split(a):
    high = a.astype(BF16)
    return high, (a - high.astype(F32)).astype(BF16)


def mm(a, b):
    ah, al = a
    bh, bl = b
    return dot(ah, bh) + (dot(ah, bl) + dot(al, bh))


def mm_square(a, b):
    ah, al = a
    bh, bl = b
    right = jnp.concatenate(
        [jnp.concatenate([bh, bl], 1), jnp.concatenate([bh, jnp.zeros_like(bl)], 1)], 0
    )
    both = dot(jnp.concatenate([ah, al], 1), right)
    width = bh.shape[1]
    return both[:, :width] + both[:, width:]


def mm_exact(a, b):
    return dot(jnp.concatenate(a, 1), jnp.concatenate([b, b], 0))


def tile_inverse(low, size):
    lane = lax.broadcasted_iota(jnp.int32, (TILE, size), 1)
    sub = lax.broadcasted_iota(jnp.int32, (TILE, size), 0)
    tile = lane // TILE
    packed = low[:TILE]
    for g in range(1, size // TILE):
        packed = jnp.where(tile == g, low[g * TILE : (g + 1) * TILE], packed)
    inner = lane - tile * TILE
    packed = jnp.where(sub > inner, packed, 0.0)
    x = jnp.where(sub == inner, 1.0, 0.0)
    for c in range(TILE - 1):
        column = jnp.take_along_axis(packed, tile * TILE + c, axis=1)
        x = x - column * x[c : c + 1]
    return jnp.concatenate(
        [jnp.where(tile == g, x, 0.0) for g in range(size // TILE)], 0
    )


def unit_lower_inverse(lowers, size, row, col):
    apart = row ^ col
    inverses = [tile_inverse(low, size) for low in lowers]
    width = TILE
    while width < size:
        mask = (apart >= width) & (apart < 2 * width)
        parts = [split(x) for x in inverses]
        blocks = [split(jnp.where(mask, low, 0.0)) for low in lowers]
        left = [split(mm_square(x, b)) for x, b in zip(parts, blocks)]
        inverses = [x - mm_square(l, p) for x, l, p in zip(inverses, left, parts)]
        width *= 2
    return inverses


def transitions(blocks, size, dim):
    row = lax.broadcasted_iota(jnp.int32, (size, size), 0)
    col = lax.broadcasted_iota(jnp.int32, (size, size), 1)
    aux_row = lax.broadcasted_iota(jnp.int32, (AUX, size), 0)
    staged, lowers = [], []
    for kb, vb, aux in blocks:
        gram = dot(kb, kb, NT)
        norm = jnp.sum(jnp.where(row == col, gram, 0.0), 0, keepdims=True) + EPS
        rk = lax.rsqrt(norm)
        gain = aux[1:2] * (rk * rk)
        decay = aux[0:1]
        cols = jnp.where(aux_row == AUX - 1, gain, aux).T
        lowers.append(jnp.where(row > col, gram * gain, 0.0))
        staged.append((kb, vb, gain, norm * rk / decay, decay[:, size - 1 : size], cols))
    inverses = unit_lower_inverse(lowers, size, row, col)
    eye = (row == col).astype(F32)
    results = []
    for inverse, (kb, vb, gain, unscale, last, cols) in zip(inverses, staged):
        y = mm_exact(split(inverse), kb)
        z = mm_exact(split(inverse * unscale), vb)
        pair = jnp.concatenate([y, z], 1)
        kt = kb.astype(F32).T.astype(BF16)
        moved = dot(
            jnp.concatenate([kt, kt], 1),
            jnp.concatenate(split(pair * cols[:, AUX - 1 : AUX]), 0),
        )
        turn, write = last * (eye - moved[:, :dim]), last * moved[:, dim:]
        results.append((turn, write, pair, cols, gain))
    return results


def local_reads(qb, kb, pair, cols, gain):
    size = qb.shape[0]
    dim = qb.shape[1]
    row = lax.broadcasted_iota(jnp.int32, (size, size), 0)
    col = lax.broadcasted_iota(jnp.int32, (size, size), 1)
    q = qb.astype(F32)
    scale = lax.rsqrt(jnp.sum(q * q, -1, keepdims=True) + EPS) * cols[:, 0:1]
    scores = jnp.where(row >= col, dot(qb, kb, NT) * gain, 0.0)
    seen = mm(split(scores), split(pair))
    return scale * (q - seen[:, :dim]), (scale * cols[:, 2:3]) * seen[:, dim:]


def chain(upper, lower):
    return mm_square(split(upper), split(lower))


def beside(turn, write):
    th, tl = split(turn)
    wh, wl = split(write)
    return jnp.concatenate([th, wh], 1), jnp.concatenate([tl, wl], 1)


def kernel(n_grp, n_seq, heads, *refs):
    q_ref, k_ref, v_ref, f_ref, b_ref, w_ref, out_ref = refs[:7]
    (
        aux,
        kv_out,
        q_out,
        kv_in,
        q_in,
        pairs,
        colb,
        gains,
        turns,
        writes,
        node_t,
        node_w,
        low_t,
        low_w,
        r_out,
        r_in,
        colr,
        near,
        near_in,
        far,
        far_in,
        mid_t,
        mid_w,
        top_t,
        top_w,
    ) = refs[7:32]
    (
        s_kv,
        r_kv,
        s_q,
        r_q,
        s_node,
        r_node,
        s_r,
        r_r,
        s_mid,
        r_mid,
        s_top,
        r_top,
        s_near,
        r_near,
        s_far,
        r_far,
    ) = refs[32:]
    total_bits = (n_grp * n_seq).bit_length() - 1
    middle = list(range(2, total_bits - 2))
    xl, yl = total_bits - 2, total_bits - 1
    n_mid = len(middle)
    size = q_ref.shape[0]
    dim = q_ref.shape[1] // heads
    slots = heads // 2
    waves = slots // 2
    pos = lax.axis_index("grp") * n_seq + lax.axis_index("seq")

    def bit_of(l):
        return (pos // (1 << l)) % 2

    def where_is(number):
        return (number // n_seq, number % n_seq)

    def flipped(*ls):
        return where_is(pos + sum((1 - 2 * bit_of(l)) * (1 << l) for l in ls))

    def columns(i):
        return pl.ds(pl.multiple_of(i * dim, dim), dim)

    def remote(source, target, send, receive, device):
        return pltpu.make_async_remote_copy(
            src_ref=source,
            dst_ref=target,
            send_sem=send,
            recv_sem=receive,
            device_id=device,
            device_id_type=MESH,
        )

    core, zl, xx, yy = bit_of(0), bit_of(1), bit_of(xl), bit_of(yl)
    other = 1 - core
    beside_me, across, diagonal = flipped(0), flipped(1), flipped(0, 1)
    tops = (flipped(xl), flipped(yl), flipped(xl, yl))
    mine = 2 * yy + xx
    theirs = (2 * yy + 1 - xx, 2 * (1 - yy) + xx, 2 * (1 - yy) + 1 - xx)
    greeted = [beside_me, across, diagonal, *tops] + [flipped(l) for l in middle]
    barrier = pltpu.get_barrier_semaphore()
    for device in greeted:
        pl.semaphore_signal(barrier, inc=1, device_id=device, device_id_type=MESH)

    total = f_ref[...]
    lane = lax.broadcasted_iota(jnp.int32, total.shape, 1)
    step = 1
    while step < size:
        total = total + jnp.where(lane >= step, pltpu.roll(total, step, 1), 0.0)
        step *= 2
    decay = jnp.exp(-total)
    aux[...] = jnp.zeros_like(aux)
    levels = w_ref.shape[0]
    for h in range(heads):
        aux[h, 0:1] = decay[h : h + 1]
        aux[h, 1:2] = b_ref[h : h + 1]
        for l in range(levels):
            aux[h, 2 + l : 3 + l] = w_ref[l, h : h + 1]

    for j in range(slots):
        h = other * slots + j
        kv_out[j, :size] = k_ref[:, columns(h)].astype(F32)
        kv_out[j, size : 2 * size] = v_ref[:, columns(h)].astype(F32)
        kv_out[j, 2 * size :] = aux[h]
        q_out[j] = q_ref[:, columns(h)].astype(F32)
    pl.semaphore_wait(barrier, len(greeted))

    pending = []

    def begin(copy):
        copy.start()
        pending.append(copy)
        return copy

    kv_copies = [
        begin(remote(kv_out.at[j], kv_in.at[j], s_kv.at[j], r_kv.at[j], beside_me))
        for j in range(slots)
    ]
    q_copies = [
        begin(remote(q_out.at[j], q_in.at[j], s_q.at[j], r_q.at[j], beside_me))
        for j in range(slots)
    ]

    def own_block(j):
        h = core * slots + j
        return k_ref[:, columns(h)], v_ref[:, columns(h)], aux[h]

    def other_block(j):
        return (
            kv_in[j, :size].astype(BF16),
            kv_in[j, size : 2 * size].astype(BF16),
            kv_in[j, 2 * size :],
        )

    def solve(work):
        done = transitions(
            [own_block(j) if e == 0 else other_block(j) for j, e in work], size, dim
        )
        for (j, e), (turn, write, pair, cols, gain) in zip(work, done):
            s = other if e else core
            turns[s, j] = turn
            writes[s, j] = write
            pairs[e, j] = pair
            colb[e, j] = cols
            gains[e, j] = jnp.broadcast_to(gain, (8, size))

    node_copies = [
        [
            remote(
                source.at[2 * u + 1 - zl],
                target.at[u, zl],
                s_node.at[2 * u + n],
                r_node.at[2 * u + n],
                across,
            )
            for n, (source, target) in enumerate(((node_t, low_t), (node_w, low_w)))
        ]
        for u in range(waves)
    ]
    pending += [copy for copies in node_copies for copy in copies]

    def send_nodes(u):
        for copy in node_copies[u]:
            copy.start()

    def merge(u):
        for j in (2 * u, 2 * u + 1):
            upper = turns[1, j]
            node_t[j] = chain(upper, turns[0, j])
            node_w[j] = chain(upper, writes[0, j]) + writes[1, j]
        low_t[u, zl] = node_t[2 * u + zl]
        low_w[u, zl] = node_w[2 * u + zl]

    def send_mid(m, u, n):
        l = middle[m]
        ref = (mid_t, mid_w)[n].at[m, u, bit_of(l)]
        begin(remote(ref, ref, s_mid.at[m, 2 * u + n], r_mid.at[m, 2 * u + n], flipped(l)))

    def wait_mid(m, u, n):
        l = middle[m]
        ref = (mid_t, mid_w)[n].at[m, u, 1 - bit_of(l)]
        remote(
            ref, ref, s_mid.at[m, 2 * u + n], r_mid.at[m, 2 * u + n], flipped(l)
        ).wait_recv()

    def send_top(u, n):
        ref = (top_t, top_w)[n].at[u, mine]
        for p in range(3):
            i = 4 * p + 2 * u + n
            begin(remote(ref, ref, s_top.at[i], r_top.at[i], tops[p]))

    def wait_top(u, n):
        for p in range(3):
            ref = (top_t, top_w)[n].at[u, theirs[p]]
            i = 4 * p + 2 * u + n
            remote(ref, ref, s_top.at[i], r_top.at[i], tops[p]).wait_recv()

    def lift(m, u, n):
        if m < 0:
            node_copies[u][n].wait_recv()
            ts, ws = low_t.at[u], low_w.at[u]
        else:
            wait_mid(m, u, n)
            ts, ws = mid_t.at[m, u], mid_w.at[m, u]
        value = chain(ts[1], ts[0]) if n == 0 else chain(ts[1], ws[0]) + ws[1]
        if m + 1 < n_mid:
            (mid_t, mid_w)[n][m + 1, u, bit_of(middle[m + 1])] = value
            send_mid(m + 1, u, n)
        else:
            (top_t, top_w)[n][u, mine] = value
            send_top(u, n)

    def reads(group):
        for j in group:
            q_copies[j].wait_recv()
        for j in group:
            h = core * slots + j
            for e in range(2):
                if e == 0:
                    qb, kb = q_ref[:, columns(h)], k_ref[:, columns(h)]
                else:
                    qb, kb = q_in[j].astype(BF16), kv_in[j, :size].astype(BF16)
                s = other if e else core
                r, inside = local_reads(qb, kb, pairs[e, j], colb[e, j], gains[e, j, :1])
                r_out[j, s, :size] = r
                r_out[j, s, size:] = (kv_in[j, 2 * size :] if e else aux[h])[4 : 4 + ROWS]
                near[j, s] = inside
        for j in group:
            seen = mm(split(r_out[j, 1, :size]), beside(turns[0, j], writes[0, j]))
            weight = jnp.where(core == 1, colb[0, j], colb[1, j])[:, 3:4]
            r_out[j, 1, :size] = seen[:, :dim]
            near[j, 1] += weight * seen[:, dim:]

    r_copies = {}

    def send_reads(u):
        j = 2 * u + 1 - zl
        for s in range(2):
            i = 2 * u + s
            r_copies[u, s] = begin(
                remote(r_out.at[j, s], r_in.at[u, zl, s], s_r.at[i], r_r.at[i], across)
            )
            r_in[u, zl, s] = r_out[2 * u + zl, s]

    def read(u, items, lower, l, gate=None, fresh=False):
        rows = jnp.concatenate([r_in[u, z, s, :size] for z, s in items], 0)
        seen = mm(split(rows), lower)
        for n, (z, s) in enumerate(items):
            part = seen[n * size : (n + 1) * size]
            value = colr[u, z, s][:, l - 1 : l] * part[:, dim:]
            if gate is not None:
                value = jnp.where(gate, value, 0.0)
            far[u, z, s] = value if fresh else far[u, z, s] + value
            new = part[:, :dim]
            r_in[u, z, s, :size] = (
                new if gate is None else jnp.where(gate, new, r_in[u, z, s, :size])
            )

    everyone = [(z, s) for z in range(2) for s in range(2)]

    def low_reads(u):
        for s in range(2):
            r_copies[u, s].wait_recv()
        for z, s in everyone:
            colr[u, z, s] = r_in[u, z, s, size:].T
        for s in range(2):
            far[u, 0, s] = jnp.zeros((size, dim), F32)
        read(u, everyone[2:], beside(low_t[u, 0], low_w[u, 0]), 1, fresh=True)

    def mid_reads(u):
        for m, l in enumerate(middle):
            read(u, everyone, beside(mid_t[m, u, 0], mid_w[m, u, 0]), l, bit_of(l) == 1)

    far_copies = []

    def top_reads(u):
        wait_top(u, 0)
        wait_top(u, 1)
        state = chain(top_t[u, 1], top_w[u, 0]) + top_w[u, 1]
        read(u, everyone, beside(top_t[u, 2 * yy], top_w[u, 2 * yy]), xl, xx == 1)
        lower = split(state)
        gate = yy == 1
        for z, s, device in (
            (1 - zl, core, across),
            (1 - zl, other, diagonal),
            (zl, other, beside_me),
            (zl, core, None),
        ):
            seen = mm(split(r_in[u, z, s, :size]), lower)
            weight = colr[u, z, s][:, yl - 1 : yl]
            far[u, z, s] += jnp.where(gate, weight * seen, 0.0)
            h = core * slots + 2 * u + zl
            if device is None:
                far_in[h] = far[u, zl, core]
                continue
            i = 3 * u + len(far_copies) % 3
            far_copies.append(
                begin(remote(far.at[u, z, s], far_in.at[h], s_far.at[i], r_far.at[i], device))
            )

    solve([(0, 0), (1, 0)])
    for j in (0, 1):
        kv_copies[j].wait_recv()
    solve([(0, 1), (1, 1)])
    merge(0)
    send_nodes(0)
    for j in range(2, slots):
        kv_copies[j].wait_recv()
    solve([(j, e) for j in (2, 3) for e in range(2)])
    merge(1)
    send_nodes(1)
    lift(-1, 0, 0)
    lift(-1, 0, 1)
    reads((0, 1))
    reads((2, 3))
    lift(-1, 1, 0)
    lift(-1, 1, 1)
    for u in range(waves):
        send_reads(u)
    near_copies = [
        begin(
            remote(near.at[j, other], near_in.at[j], s_near.at[j], r_near.at[j], beside_me)
        )
        for j in range(slots)
    ]
    for m in range(n_mid - 1):
        for u in range(waves):
            lift(m, u, 0)
            lift(m, u, 1)
    for u in range(waves):
        lift(n_mid - 1, u, 0)
        lift(n_mid - 1, u, 1)
    for u in range(waves):
        low_reads(u)
        mid_reads(u)
        top_reads(u)

    for copy in near_copies:
        copy.wait_recv()
    for u in range(waves):
        for n, (c, z) in enumerate(((core, 1 - zl), (other, 1 - zl), (other, zl), (core, zl))):
            j = 2 * u + z
            h = c * slots + j
            if n < 3:
                i = 3 * u + n
                device = (across, diagonal, beside_me)[n]
                remote(
                    far.at[u, zl, core], far_in.at[h], s_far.at[i], r_far.at[i], device
                ).wait_recv()
            here = near[j, core] if n in (0, 3) else near_in[j]
            out_ref[:, columns(h)] = here + far_in[h]
    for copy in pending:
        copy.wait_send()


def on_device(n_grp, n_seq, queries, keys, values, forget, beta, level_weights):
    size = queries.shape[0]
    heads = forget.shape[1]
    dim = queries.shape[1] // heads
    slots = heads // 2
    n_mid = (n_grp * n_seq).bit_length() - 5
    dma = pltpu.SemaphoreType.DMA

    def vmem(*shape):
        return pltpu.VMEM(shape, F32)

    return pl.pallas_call(
        functools.partial(kernel, n_grp, n_seq, heads),
        out_shape=pltpu.VMEM((size, heads * dim), F32),
        in_specs=[pl.BlockSpec(memory_space=pltpu.VMEM)] * 6,
        out_specs=pl.BlockSpec(memory_space=pltpu.VMEM),
        scratch_shapes=[
            vmem(heads, AUX, size),
            vmem(slots, 2 * size + AUX, dim),
            vmem(slots, size, dim),
            vmem(slots, 2 * size + AUX, dim),
            vmem(slots, size, dim),
            vmem(2, slots, size, 2 * dim),
            vmem(2, slots, size, AUX),
            vmem(2, slots, 8, size),
        ]
        + [vmem(2, slots, dim, dim)] * 2
        + [vmem(slots, dim, dim)] * 2
        + [vmem(2, 2, dim, dim)] * 2
        + [
            vmem(slots, 2, size + ROWS, dim),
            vmem(2, 2, 2, size + ROWS, dim),
            vmem(2, 2, 2, size, ROWS),
            vmem(slots, 2, size, dim),
            vmem(slots, size, dim),
            vmem(2, 2, 2, size, dim),
            vmem(heads, size, dim),
        ]
        + [vmem(n_mid, 2, 2, dim, dim)] * 2
        + [vmem(2, 4, dim, dim)] * 2
        + [dma((slots,))] * 4
        + [dma((4,))] * 4
        + [dma((n_mid, 4))] * 2
        + [dma((12,))] * 2
        + [dma((slots,))] * 2
        + [dma((6,))] * 2,
        compiler_params=pltpu.CompilerParams(collective_id=0, has_side_effects=True),
    )(
        queries,
        keys,
        values,
        forget.T,
        beta.T,
        jnp.transpose(level_weights, (0, 2, 1)),
    )


def solution(mesh):
    both = P(("grp", "seq"), None)
    return jax.shard_map(
        functools.partial(on_device, mesh.shape["grp"], mesh.shape["seq"]),
        mesh=mesh,
        in_specs=(both, both, both, both, both, P(None, ("grp", "seq"), None)),
        out_specs=both,
        check_vma=False,
    )
```

```python
import functools

import jax
import jax.numpy as jnp
from jax import lax
from jax.experimental import pallas as pl
from jax.experimental.pallas import tpu as pltpu
from jax.sharding import PartitionSpec as P

MESH = pl.DeviceIdType.MESH
F32 = jnp.float32
BF16 = jnp.bfloat16
NN = (((1,), (0,)), ((), ()))
NT = (((1,), (1,)), ((), ()))
AUX = 16
ROWS = 8
TILE = 16
EPS = 1e-06


def dot(a, b, dims=NN):
    return lax.dot_general(a, b, dims, preferred_element_type=F32)


def split(a):
    high = a.astype(BF16)
    return high, (a - high.astype(F32)).astype(BF16)


def mm(a, b):
    ah, al = a
    bh, bl = b
    return dot(ah, bh) + (dot(ah, bl) + dot(al, bh))


def mm_square(a, b):
    ah, al = a
    bh, bl = b
    right = jnp.concatenate(
        [jnp.concatenate([bh, bl], 1), jnp.concatenate([bh, jnp.zeros_like(bl)], 1)], 0
    )
    both = dot(jnp.concatenate([ah, al], 1), right)
    width = bh.shape[1]
    return both[:, :width] + both[:, width:]


def mm_exact(a, b):
    return dot(jnp.concatenate(a, 1), jnp.concatenate([b, b], 0))


def tile_inverse(low, size):
    lane = lax.broadcasted_iota(jnp.int32, (TILE, size), 1)
    sub = lax.broadcasted_iota(jnp.int32, (TILE, size), 0)
    tile = lane // TILE
    packed = low[:TILE]
    for g in range(1, size // TILE):
        packed = jnp.where(tile == g, low[g * TILE : (g + 1) * TILE], packed)
    inner = lane - tile * TILE
    packed = jnp.where(sub > inner, packed, 0.0)
    x = jnp.where(sub == inner, 1.0, 0.0)
    for c in range(TILE - 1):
        column = jnp.take_along_axis(packed, tile * TILE + c, axis=1)
        x = x - column * x[c : c + 1]
    return jnp.concatenate(
        [jnp.where(tile == g, x, 0.0) for g in range(size // TILE)], 0
    )


def unit_lower_inverse(lowers, size, row, col):
    apart = row ^ col
    inverses = [tile_inverse(low, size) for low in lowers]
    width = TILE
    while width < size:
        mask = (apart >= width) & (apart < 2 * width)
        parts = [split(x) for x in inverses]
        blocks = [split(jnp.where(mask, low, 0.0)) for low in lowers]
        left = [split(mm_square(x, b)) for x, b in zip(parts, blocks)]
        inverses = [x - mm_square(l, p) for x, l, p in zip(inverses, left, parts)]
        width *= 2
    return inverses


def transitions(blocks, size, dim):
    row = lax.broadcasted_iota(jnp.int32, (size, size), 0)
    col = lax.broadcasted_iota(jnp.int32, (size, size), 1)
    aux_row = lax.broadcasted_iota(jnp.int32, (AUX, size), 0)
    staged, lowers = [], []
    for kb, vb, aux in blocks:
        gram = dot(kb, kb, NT)
        norm = jnp.sum(jnp.where(row == col, gram, 0.0), 0, keepdims=True) + EPS
        rk = lax.rsqrt(norm)
        gain = aux[1:2] * (rk * rk)
        decay = aux[0:1]
        cols = jnp.where(aux_row == AUX - 1, gain, aux).T
        lowers.append(jnp.where(row > col, gram * gain, 0.0))
        staged.append((kb, vb, gain, norm * rk / decay, decay[:, size - 1 : size], cols))
    inverses = unit_lower_inverse(lowers, size, row, col)
    eye = (row == col).astype(F32)
    results = []
    for inverse, (kb, vb, gain, unscale, last, cols) in zip(inverses, staged):
        y = mm_exact(split(inverse), kb)
        z = mm_exact(split(inverse * unscale), vb)
        pair = jnp.concatenate([y, z], 1)
        kt = kb.astype(F32).T.astype(BF16)
        moved = dot(
            jnp.concatenate([kt, kt], 1),
            jnp.concatenate(split(pair * cols[:, AUX - 1 : AUX]), 0),
        )
        turn, write = last * (eye - moved[:, :dim]), last * moved[:, dim:]
        results.append((turn, write, pair, cols, gain))
    return results


def local_reads(qb, kb, pair, cols, gain):
    size = qb.shape[0]
    dim = qb.shape[1]
    row = lax.broadcasted_iota(jnp.int32, (size, size), 0)
    col = lax.broadcasted_iota(jnp.int32, (size, size), 1)
    q = qb.astype(F32)
    scale = lax.rsqrt(jnp.sum(q * q, -1, keepdims=True) + EPS) * cols[:, 0:1]
    scores = jnp.where(row >= col, dot(qb, kb, NT) * gain, 0.0)
    seen = mm(split(scores), split(pair))
    return scale * (q - seen[:, :dim]), (scale * cols[:, 2:3]) * seen[:, dim:]


def chain(upper, lower):
    return mm_square(split(upper), split(lower))


def beside(turn, write):
    th, tl = split(turn)
    wh, wl = split(write)
    return jnp.concatenate([th, wh], 1), jnp.concatenate([tl, wl], 1)


def kernel(n_grp, n_seq, heads, *refs):
    arguments, out_ref = refs[:6], refs[6]
    (
        aux,
        kv_out,
        q_out,
        kv_in,
        q_in,
        pairs,
        colb,
        gains,
        turns,
        writes,
        node_t,
        node_w,
        low_t,
        low_w,
        r_out,
        r_in,
        colr,
        near,
        near_in,
        far,
        far_in,
        mid_t,
        mid_w,
        top_t,
        top_w,
        *held,
    ) = refs[7:38]
    q_ref, k_ref, v_ref, f_ref, b_ref, w_ref = held
    (
        s_kv,
        r_kv,
        s_q,
        r_q,
        s_node,
        r_node,
        s_r,
        r_r,
        s_mid,
        r_mid,
        s_top,
        r_top,
        s_near,
        r_near,
        s_far,
        r_far,
        s_load,
    ) = refs[38:]
    total_bits = (n_grp * n_seq).bit_length() - 1
    middle = list(range(2, total_bits - 2))
    xl, yl = total_bits - 2, total_bits - 1
    n_mid = len(middle)
    size = q_ref.shape[0]
    dim = q_ref.shape[1] // heads
    slots = heads // 2
    waves = slots // 2
    pos = lax.axis_index("grp") * n_seq + lax.axis_index("seq")

    def bit_of(l):
        return (pos // (1 << l)) % 2

    def where_is(number):
        return (number // n_seq, number % n_seq)

    def flipped(*ls):
        return where_is(pos + sum((1 - 2 * bit_of(l)) * (1 << l) for l in ls))

    def columns(i):
        return pl.ds(pl.multiple_of(i * dim, dim), dim)

    def remote(source, target, send, receive, device):
        return pltpu.make_async_remote_copy(
            src_ref=source,
            dst_ref=target,
            send_sem=send,
            recv_sem=receive,
            device_id=device,
            device_id_type=MESH,
        )

    core, zl, xx, yy = bit_of(0), bit_of(1), bit_of(xl), bit_of(yl)
    other = 1 - core
    beside_me, across, diagonal = flipped(0), flipped(1), flipped(0, 1)
    tops = (flipped(xl), flipped(yl), flipped(xl, yl))
    mine = 2 * yy + xx
    theirs = (2 * yy + 1 - xx, 2 * (1 - yy) + xx, 2 * (1 - yy) + 1 - xx)
    greeted = [beside_me, across, diagonal, *tops] + [flipped(l) for l in middle]
    barrier = pltpu.get_barrier_semaphore()
    for device in greeted:
        pl.semaphore_signal(barrier, inc=1, device_id=device, device_id_type=MESH)

    loads = [
        pltpu.make_async_copy(source, target, s_load.at[i])
        for i, (source, target) in enumerate(zip(arguments, held))
    ]
    for i in (3, 4, 5, 1, 2, 0):
        loads[i].start()
    for i in (3, 4, 5):
        loads[i].wait()

    total = f_ref[...]
    lane = lax.broadcasted_iota(jnp.int32, total.shape, 1)
    step = 1
    while step < size:
        total = total + jnp.where(lane >= step, pltpu.roll(total, step, 1), 0.0)
        step *= 2
    decay = jnp.exp(-total)
    aux[...] = jnp.zeros_like(aux)
    levels = w_ref.shape[0]
    for h in range(heads):
        aux[h, 0:1] = decay[h : h + 1]
        aux[h, 1:2] = b_ref[h : h + 1]
        for l in range(levels):
            aux[h, 2 + l : 3 + l] = w_ref[l, h : h + 1]

    away = [2 * u + 1 - zl for u in range(waves)]
    kept = [2 * u + zl for u in range(waves)]
    loads[1].wait()
    loads[2].wait()
    for j in away + kept:
        h = other * slots + j
        kv_out[j, :size] = k_ref[:, columns(h)].astype(F32)
        kv_out[j, size : 2 * size] = v_ref[:, columns(h)].astype(F32)
        kv_out[j, 2 * size :] = aux[h]
    pl.semaphore_wait(barrier, len(greeted))

    pending = []

    def begin(copy):
        copy.start()
        pending.append(copy)
        return copy

    def kv_copy(j):
        return remote(kv_out.at[j], kv_in.at[j], s_kv.at[j], r_kv.at[j], beside_me)

    def q_copy(j):
        return remote(q_out.at[j], q_in.at[j], s_q.at[j], r_q.at[j], beside_me)

    for j in away + kept:
        begin(kv_copy(j))

    def own_block(j):
        h = core * slots + j
        return k_ref[:, columns(h)], v_ref[:, columns(h)], aux[h]

    def other_block(j):
        return (
            kv_in[j, :size].astype(BF16),
            kv_in[j, size : 2 * size].astype(BF16),
            kv_in[j, 2 * size :],
        )

    def solve(work):
        done = transitions(
            [own_block(j) if e == 0 else other_block(j) for j, e in work], size, dim
        )
        for (j, e), (turn, write, pair, cols, gain) in zip(work, done):
            s = other if e else core
            turns[s, j] = turn
            writes[s, j] = write
            pairs[e, j] = pair
            colb[e, j] = cols
            gains[e, j] = jnp.broadcast_to(gain, (8, size))

    node_copies = [
        [
            remote(
                source.at[2 * u + 1 - zl],
                target.at[u, zl],
                s_node.at[2 * u + n],
                r_node.at[2 * u + n],
                across,
            )
            for n, (source, target) in enumerate(((node_t, low_t), (node_w, low_w)))
        ]
        for u in range(waves)
    ]
    pending += [copy for copies in node_copies for copy in copies]

    def send_nodes(u):
        for copy in node_copies[u]:
            copy.start()

    def merge(j):
        upper = turns[1, j]
        node_t[j] = chain(upper, turns[0, j])
        node_w[j] = chain(upper, writes[0, j]) + writes[1, j]

    def send_mid(m, u, n):
        l = middle[m]
        ref = (mid_t, mid_w)[n].at[m, u, bit_of(l)]
        begin(remote(ref, ref, s_mid.at[m, 2 * u + n], r_mid.at[m, 2 * u + n], flipped(l)))

    def wait_mid(m, u, n):
        l = middle[m]
        ref = (mid_t, mid_w)[n].at[m, u, 1 - bit_of(l)]
        remote(
            ref, ref, s_mid.at[m, 2 * u + n], r_mid.at[m, 2 * u + n], flipped(l)
        ).wait_recv()

    first_x, second_x = xx == 0, xx == 1
    first_y, second_y = yy == 0, yy == 1

    def top_copy(u, n, p, group):
        ref = (top_t, top_w)[n].at[u, group]
        i = 4 * p + 2 * u + n
        return remote(ref, ref, s_top.at[i], r_top.at[i], tops[p])

    def each_top(u, n, act):
        def do(*ps):
            def run():
                for p in ps:
                    act(top_copy(u, n, p, mine))

            return run

        if n == 1:
            pl.when(first_x)(do(0))
            pl.when(first_y)(do(1, 2))
        else:
            pl.when(first_x & second_y)(do(0))
            pl.when(second_x & first_y)(do(1, 2))

    def send_top(u, n):
        each_top(u, n, lambda copy: copy.start())

    def wait_top(u, n, p):
        top_copy(u, n, p, theirs[p]).wait_recv()

    def lift(m, u, n):
        if m < 0:
            node_copies[u][n].wait_recv()
            ts, ws = low_t.at[u], low_w.at[u]
        else:
            wait_mid(m, u, n)
            ts, ws = mid_t.at[m, u], mid_w.at[m, u]
        value = chain(ts[1], ts[0]) if n == 0 else chain(ts[1], ws[0]) + ws[1]
        if m + 1 < n_mid:
            (mid_t, mid_w)[n][m + 1, u, bit_of(middle[m + 1])] = value
            send_mid(m + 1, u, n)
        else:
            (top_t, top_w)[n][u, mine] = value
            send_top(u, n)

    def reads(group):
        for j in group:
            q_copy(j).wait_recv()
        for j in group:
            h = core * slots + j
            for e in range(2):
                if e == 0:
                    qb, kb = q_ref[:, columns(h)], k_ref[:, columns(h)]
                else:
                    qb, kb = q_in[j].astype(BF16), kv_in[j, :size].astype(BF16)
                s = other if e else core
                r, inside = local_reads(qb, kb, pairs[e, j], colb[e, j], gains[e, j, :1])
                r_out[j, s, :size] = r
                r_out[j, s, size:] = (kv_in[j, 2 * size :] if e else aux[h])[4 : 4 + ROWS]
                near[j, s] = inside
        for j in group:
            seen = mm(split(r_out[j, 1, :size]), beside(turns[0, j], writes[0, j]))
            weight = jnp.where(core == 1, colb[0, j], colb[1, j])[:, 3:4]
            r_out[j, 1, :size] = seen[:, :dim]
            near[j, 1] += weight * seen[:, dim:]

    r_copies = {}

    def send_reads(u):
        j = 2 * u + 1 - zl
        for s in range(2):
            i = 2 * u + s
            r_copies[u, s] = begin(
                remote(r_out.at[j, s], r_in.at[u, zl, s], s_r.at[i], r_r.at[i], across)
            )
            r_in[u, zl, s] = r_out[2 * u + zl, s]

    def read(u, items, lower, l, fresh=False):
        rows = jnp.concatenate([r_in[u, z, s, :size] for z, s in items], 0)
        seen = mm(split(rows), lower)
        for n, (z, s) in enumerate(items):
            part = seen[n * size : (n + 1) * size]
            value = colr[u, z, s][:, l - 1 : l] * part[:, dim:]
            far[u, z, s] = value if fresh else far[u, z, s] + value
            r_in[u, z, s, :size] = part[:, :dim]

    everyone = [(z, s) for z in range(2) for s in range(2)]

    def low_reads(u):
        for s in range(2):
            r_copies[u, s].wait_recv()
        for z, s in everyone:
            colr[u, z, s] = r_in[u, z, s, size:].T
        for s in range(2):
            far[u, 0, s] = jnp.zeros((size, dim), F32)
        read(u, everyone[2:], beside(low_t[u, 0], low_w[u, 0]), 1, fresh=True)

    def mid_reads(u):
        for m, l in enumerate(middle):

            @pl.when(bit_of(l) == 1)
            def _():
                read(u, everyone, beside(mid_t[m, u, 0], mid_w[m, u, 0]), l)

    def far_copy(u, n):
        z, s, device = (
            (1 - zl, core, across),
            (1 - zl, other, diagonal),
            (zl, other, beside_me),
        )[n]
        h = core * slots + 2 * u + zl
        i = 3 * u + n
        return remote(far.at[u, z, s], far_in.at[h], s_far.at[i], r_far.at[i], device)

    def top_reads(u):
        @pl.when(second_x)
        def _():
            wait_top(u, 1, 0)
            pl.when(second_y)(functools.partial(wait_top, u, 0, 0))
            read(u, everyone, beside(top_t[u, 2 * yy], top_w[u, 2 * yy]), xl)

        @pl.when(second_y)
        def _():
            pl.when(second_x)(functools.partial(wait_top, u, 0, 1))
            pl.when(first_x)(functools.partial(wait_top, u, 0, 2))
            wait_top(u, 1, 1)
            wait_top(u, 1, 2)
            lower = split(chain(top_t[u, 1], top_w[u, 0]) + top_w[u, 1])
            for n, (z, s) in enumerate(
                ((1 - zl, core), (1 - zl, other), (zl, other), (zl, core))
            ):
                seen = mm(split(r_in[u, z, s, :size]), lower)
                far[u, z, s] += colr[u, z, s][:, yl - 1 : yl] * seen
                if n < 3:
                    far_copy(u, n).start()

        @pl.when(first_y)
        def _():
            for n in range(3):
                far_copy(u, n).start()

        far_in[core * slots + 2 * u + zl] = far[u, zl, core]

    solve([(j, 0) for j in away])
    loads[0].wait()
    for j in range(slots):
        q_out[j] = q_ref[:, columns(other * slots + j)].astype(F32)
    for j in range(slots):
        begin(q_copy(j))
    for j in away:
        kv_copy(j).wait_recv()
    solve([(j, 1) for j in away])
    for u in range(waves):
        merge(away[u])
        send_nodes(u)
    for j in kept:
        kv_copy(j).wait_recv()
    solve([(j, e) for j in kept for e in range(2)])
    for u in range(waves):
        merge(kept[u])
        low_t[u, zl] = node_t[kept[u]]
        low_w[u, zl] = node_w[kept[u]]
    lift(-1, 0, 0)
    lift(-1, 0, 1)
    reads((0, 1))
    reads((2, 3))
    lift(-1, 1, 0)
    lift(-1, 1, 1)
    for u in range(waves):
        send_reads(u)
    near_copies = [
        begin(
            remote(near.at[j, other], near_in.at[j], s_near.at[j], r_near.at[j], beside_me)
        )
        for j in range(slots)
    ]
    for m in range(n_mid - 1):
        for u in range(waves):
            lift(m, u, 0)
            lift(m, u, 1)
    for u in range(waves):
        lift(n_mid - 1, u, 0)
        lift(n_mid - 1, u, 1)
    for u in range(waves):
        low_reads(u)
        mid_reads(u)
        top_reads(u)

    for copy in near_copies:
        copy.wait_recv()
    for u in range(waves):
        for n, (c, z) in enumerate(((core, 1 - zl), (other, 1 - zl), (other, zl), (core, zl))):
            j = 2 * u + z
            h = c * slots + j
            if n < 3:
                i = 3 * u + n
                device = (across, diagonal, beside_me)[n]
                remote(
                    far.at[u, zl, core], far_in.at[h], s_far.at[i], r_far.at[i], device
                ).wait_recv()
            here = near[j, core] if n in (0, 3) else near_in[j]
            out_ref[:, columns(h)] = here + far_in[h]
    for copy in pending:
        copy.wait_send()
    for u in range(waves):
        for n in range(3):
            far_copy(u, n).wait_send()
        for n in range(2):
            each_top(u, n, lambda copy: copy.wait_send())


def on_device(n_grp, n_seq, queries, keys, values, forget, beta, level_weights):
    size = queries.shape[0]
    heads = forget.shape[1]
    dim = queries.shape[1] // heads
    slots = heads // 2
    n_mid = (n_grp * n_seq).bit_length() - 5
    dma = pltpu.SemaphoreType.DMA
    small = forget.T, beta.T, jnp.transpose(level_weights, (0, 2, 1))
    arguments = (queries, keys, values, *small)

    def vmem(*shape):
        return pltpu.VMEM(shape, F32)

    return pl.pallas_call(
        functools.partial(kernel, n_grp, n_seq, heads),
        out_shape=pltpu.VMEM((size, heads * dim), F32),
        in_specs=[pl.BlockSpec(memory_space=pl.ANY)] * 6,
        out_specs=pl.BlockSpec(memory_space=pltpu.VMEM),
        scratch_shapes=[
            vmem(heads, AUX, size),
            vmem(slots, 2 * size + AUX, dim),
            vmem(slots, size, dim),
            vmem(slots, 2 * size + AUX, dim),
            vmem(slots, size, dim),
            vmem(2, slots, size, 2 * dim),
            vmem(2, slots, size, AUX),
            vmem(2, slots, 8, size),
        ]
        + [vmem(2, slots, dim, dim)] * 2
        + [vmem(slots, dim, dim)] * 2
        + [vmem(2, 2, dim, dim)] * 2
        + [
            vmem(slots, 2, size + ROWS, dim),
            vmem(2, 2, 2, size + ROWS, dim),
            vmem(2, 2, 2, size, ROWS),
            vmem(slots, 2, size, dim),
            vmem(slots, size, dim),
            vmem(2, 2, 2, size, dim),
            vmem(heads, size, dim),
        ]
        + [vmem(n_mid, 2, 2, dim, dim)] * 2
        + [vmem(2, 4, dim, dim)] * 2
        + [pltpu.VMEM(a.shape, a.dtype) for a in arguments]
        + [dma((slots,))] * 4
        + [dma((4,))] * 4
        + [dma((n_mid, 4))] * 2
        + [dma((12,))] * 2
        + [dma((slots,))] * 2
        + [dma((6,))] * 3,
        compiler_params=pltpu.CompilerParams(collective_id=0, has_side_effects=True),
    )(*arguments)


def solution(mesh):
    both = P(("grp", "seq"), None)
    return jax.shard_map(
        functools.partial(on_device, mesh.shape["grp"], mesh.shape["seq"]),
        mesh=mesh,
        in_specs=(both, both, both, both, both, P(None, ("grp", "seq"), None)),
        out_specs=both,
        check_vma=False,
    )
```

```python
import functools

import jax
import jax.numpy as jnp
from jax import lax
from jax.experimental import pallas as pl
from jax.experimental.pallas import tpu as pltpu
from jax.sharding import PartitionSpec as P

MESH = pl.DeviceIdType.MESH
F32 = jnp.float32
BF16 = jnp.bfloat16
NN = (((1,), (0,)), ((), ()))
NT = (((1,), (1,)), ((), ()))
AUX = 16
ROWS = 8
TILE = 16
EPS = 1e-06


def dot(a, b, dims=NN):
    return lax.dot_general(a, b, dims, preferred_element_type=F32)


def split(a):
    high = a.astype(BF16)
    return high, (a - high.astype(F32)).astype(BF16)


def mm(a, b):
    ah, al = a
    bh, bl = b
    return dot(ah, bh) + (dot(ah, bl) + dot(al, bh))


def mm_square(a, b):
    ah, al = a
    bh, bl = b
    right = jnp.concatenate(
        [jnp.concatenate([bh, bl], 1), jnp.concatenate([bh, jnp.zeros_like(bl)], 1)], 0
    )
    both = dot(jnp.concatenate([ah, al], 1), right)
    width = bh.shape[1]
    return both[:, :width] + both[:, width:]


def mm_exact(a, b):
    return dot(jnp.concatenate(a, 1), jnp.concatenate([b, b], 0))


def tile_inverse(low, size):
    lane = lax.broadcasted_iota(jnp.int32, (TILE, size), 1)
    sub = lax.broadcasted_iota(jnp.int32, (TILE, size), 0)
    tile = lane // TILE
    packed = low[:TILE]
    for g in range(1, size // TILE):
        packed = jnp.where(tile == g, low[g * TILE : (g + 1) * TILE], packed)
    inner = lane - tile * TILE
    packed = jnp.where(sub > inner, packed, 0.0)
    x = jnp.where(sub == inner, 1.0, 0.0)
    for c in range(TILE - 1):
        column = jnp.take_along_axis(packed, tile * TILE + c, axis=1)
        x = x - column * x[c : c + 1]
    return jnp.concatenate(
        [jnp.where(tile == g, x, 0.0) for g in range(size // TILE)], 0
    )


def unit_lower_inverse(lowers, size, row, col):
    apart = row ^ col
    inverses = [tile_inverse(low, size) for low in lowers]
    width = TILE
    while width < size:
        mask = (apart >= width) & (apart < 2 * width)
        parts = [split(x) for x in inverses]
        blocks = [split(jnp.where(mask, low, 0.0)) for low in lowers]
        left = [split(mm_square(x, b)) for x, b in zip(parts, blocks)]
        inverses = [x - mm_square(l, p) for x, l, p in zip(inverses, left, parts)]
        width *= 2
    return inverses


def transitions(blocks, size, dim):
    row = lax.broadcasted_iota(jnp.int32, (size, size), 0)
    col = lax.broadcasted_iota(jnp.int32, (size, size), 1)
    aux_row = lax.broadcasted_iota(jnp.int32, (AUX, size), 0)
    staged, lowers = [], []
    for kb, vb, aux in blocks:
        gram = dot(kb, kb, NT)
        norm = jnp.sum(jnp.where(row == col, gram, 0.0), 0, keepdims=True) + EPS
        rk = lax.rsqrt(norm)
        gain = aux[1:2] * (rk * rk)
        decay = aux[0:1]
        cols = jnp.where(aux_row == AUX - 1, gain, aux).T
        lowers.append(jnp.where(row > col, gram * gain, 0.0))
        staged.append((kb, vb, gain, norm * rk / decay, decay[:, size - 1 : size], cols))
    inverses = unit_lower_inverse(lowers, size, row, col)
    eye = (row == col).astype(F32)
    results = []
    for inverse, (kb, vb, gain, unscale, last, cols) in zip(inverses, staged):
        y = mm_exact(split(inverse), kb)
        z = mm_exact(split(inverse * unscale), vb)
        pair = jnp.concatenate([y, z], 1)
        kt = kb.astype(F32).T.astype(BF16)
        moved = dot(
            jnp.concatenate([kt, kt], 1),
            jnp.concatenate(split(pair * cols[:, AUX - 1 : AUX]), 0),
        )
        turn, write = last * (eye - moved[:, :dim]), last * moved[:, dim:]
        results.append((turn, write, pair, cols, gain))
    return results


def local_reads(qb, kb, pair, cols, gain):
    size = qb.shape[0]
    dim = qb.shape[1]
    row = lax.broadcasted_iota(jnp.int32, (size, size), 0)
    col = lax.broadcasted_iota(jnp.int32, (size, size), 1)
    q = qb.astype(F32)
    scale = lax.rsqrt(jnp.sum(q * q, -1, keepdims=True) + EPS) * cols[:, 0:1]
    scores = jnp.where(row >= col, dot(qb, kb, NT) * gain, 0.0)
    seen = mm(split(scores), split(pair))
    return scale * (q - seen[:, :dim]), (scale * cols[:, 2:3]) * seen[:, dim:]


def chain(upper, lower):
    return mm_square(split(upper), split(lower))


def beside(turn, write):
    th, tl = split(turn)
    wh, wl = split(write)
    return jnp.concatenate([th, wh], 1), jnp.concatenate([tl, wl], 1)


def kernel(n_grp, n_seq, heads, *refs):
    arguments, out_ref = refs[:6], refs[6]
    (
        aux,
        kv_out,
        q_out,
        kv_in,
        q_in,
        pairs,
        colb,
        gains,
        turns,
        writes,
        node_t,
        node_w,
        low_t,
        low_w,
        r_out,
        r_in,
        colr,
        near,
        near_in,
        far,
        far_in,
        mid_t,
        mid_w,
        top_t,
        top_w,
        *held,
    ) = refs[7:38]
    q_ref, k_ref, v_ref, f_ref, b_ref, w_ref = held
    (
        s_kv,
        r_kv,
        s_q,
        r_q,
        s_node,
        r_node,
        s_r,
        r_r,
        s_mid,
        r_mid,
        s_top,
        r_top,
        s_near,
        r_near,
        s_far,
        r_far,
        s_load,
    ) = refs[38:]
    total_bits = (n_grp * n_seq).bit_length() - 1
    middle = list(range(2, total_bits - 2))
    xl, yl = total_bits - 2, total_bits - 1
    n_mid = len(middle)
    size = q_ref.shape[0]
    dim = q_ref.shape[1] // heads
    slots = heads // 2
    waves = slots // 2
    pos = lax.axis_index("grp") * n_seq + lax.axis_index("seq")

    def bit_of(l):
        return (pos // (1 << l)) % 2

    def where_is(number):
        return (number // n_seq, number % n_seq)

    def flipped(*ls):
        return where_is(pos + sum((1 - 2 * bit_of(l)) * (1 << l) for l in ls))

    def columns(i):
        return pl.ds(pl.multiple_of(i * dim, dim), dim)

    def remote(source, target, send, receive, device):
        return pltpu.make_async_remote_copy(
            src_ref=source,
            dst_ref=target,
            send_sem=send,
            recv_sem=receive,
            device_id=device,
            device_id_type=MESH,
        )

    core, zl, xx, yy = bit_of(0), bit_of(1), bit_of(xl), bit_of(yl)
    other = 1 - core
    beside_me, across, diagonal = flipped(0), flipped(1), flipped(0, 1)
    tops = (flipped(xl), flipped(yl), flipped(xl, yl))
    mine = 2 * yy + xx
    theirs = (2 * yy + 1 - xx, 2 * (1 - yy) + xx, 2 * (1 - yy) + 1 - xx)
    greeted = [beside_me, across, diagonal, *tops] + [flipped(l) for l in middle]
    barrier = pltpu.get_barrier_semaphore()
    for device in greeted:
        pl.semaphore_signal(barrier, inc=1, device_id=device, device_id_type=MESH)

    loads = [
        pltpu.make_async_copy(source, target, s_load.at[i])
        for i, (source, target) in enumerate(zip(arguments, held))
    ]
    for i in (3, 4, 5, 1, 2, 0):
        loads[i].start()
    for i in (3, 4, 5):
        loads[i].wait()

    total = f_ref[...]
    lane = lax.broadcasted_iota(jnp.int32, total.shape, 1)
    step = 1
    while step < size:
        total = total + jnp.where(lane >= step, pltpu.roll(total, step, 1), 0.0)
        step *= 2
    decay = jnp.exp(-total)
    aux[...] = jnp.zeros_like(aux)
    levels = w_ref.shape[0]
    for h in range(heads):
        aux[h, 0:1] = decay[h : h + 1]
        aux[h, 1:2] = b_ref[h : h + 1]
        for l in range(levels):
            aux[h, 2 + l : 3 + l] = w_ref[l, h : h + 1]

    away = [2 * u + 1 - zl for u in range(waves)]
    kept = [2 * u + zl for u in range(waves)]
    loads[1].wait()
    loads[2].wait()
    for j in away + kept:
        h = other * slots + j
        kv_out[j, :size] = k_ref[:, columns(h)].astype(F32)
        kv_out[j, size : 2 * size] = v_ref[:, columns(h)].astype(F32)
        kv_out[j, 2 * size :] = aux[h]
    pl.semaphore_wait(barrier, len(greeted))

    pending = []

    def begin(copy):
        copy.start()
        pending.append(copy)
        return copy

    def kv_copy(j):
        return remote(kv_out.at[j], kv_in.at[j], s_kv.at[j], r_kv.at[j], beside_me)

    def q_copy(j):
        return remote(q_out.at[j], q_in.at[j], s_q.at[j], r_q.at[j], beside_me)

    for j in away + kept:
        begin(kv_copy(j))

    def own_block(j):
        h = core * slots + j
        return k_ref[:, columns(h)], v_ref[:, columns(h)], aux[h]

    def other_block(j):
        return (
            kv_in[j, :size].astype(BF16),
            kv_in[j, size : 2 * size].astype(BF16),
            kv_in[j, 2 * size :],
        )

    def solve(work):
        done = transitions(
            [own_block(j) if e == 0 else other_block(j) for j, e in work], size, dim
        )
        for (j, e), (turn, write, pair, cols, gain) in zip(work, done):
            s = other if e else core
            turns[s, j] = turn
            writes[s, j] = write
            pairs[e, j] = pair
            colb[e, j] = cols
            gains[e, j] = jnp.broadcast_to(gain, (8, size))

    node_copies = [
        [
            remote(
                source.at[2 * u + 1 - zl],
                target.at[u, zl],
                s_node.at[2 * u + n],
                r_node.at[2 * u + n],
                across,
            )
            for n, (source, target) in enumerate(((node_t, low_t), (node_w, low_w)))
        ]
        for u in range(waves)
    ]
    pending += [copy for copies in node_copies for copy in copies]

    def send_nodes(u):
        for copy in node_copies[u]:
            copy.start()

    def merge(j):
        upper = turns[1, j]
        node_t[j] = chain(upper, turns[0, j])
        node_w[j] = chain(upper, writes[0, j]) + writes[1, j]

    def send_mid(m, u, n):
        l = middle[m]
        ref = (mid_t, mid_w)[n].at[m, u, bit_of(l)]
        begin(remote(ref, ref, s_mid.at[m, 2 * u + n], r_mid.at[m, 2 * u + n], flipped(l)))

    def wait_mid(m, u, n):
        l = middle[m]
        ref = (mid_t, mid_w)[n].at[m, u, 1 - bit_of(l)]
        remote(
            ref, ref, s_mid.at[m, 2 * u + n], r_mid.at[m, 2 * u + n], flipped(l)
        ).wait_recv()

    first_x, second_x = xx == 0, xx == 1
    first_y, second_y = yy == 0, yy == 1

    def top_copy(u, n, p, group):
        ref = (top_t, top_w)[n].at[u, group]
        i = 4 * p + 2 * u + n
        return remote(ref, ref, s_top.at[i], r_top.at[i], tops[p])

    def each_top(u, n, act):
        def do(*ps):
            def run():
                for p in ps:
                    act(top_copy(u, n, p, mine))

            return run

        if n == 1:
            pl.when(first_x)(do(0))
            pl.when(first_y)(do(1, 2))
        else:
            pl.when(first_x & second_y)(do(0))
            pl.when(second_x & first_y)(do(1, 2))

    def send_top(u, n):
        each_top(u, n, lambda copy: copy.start())

    def wait_top(u, n, p):
        top_copy(u, n, p, theirs[p]).wait_recv()

    def lift(m, u, n):
        if m < 0:
            node_copies[u][n].wait_recv()
            ts, ws = low_t.at[u], low_w.at[u]
        else:
            wait_mid(m, u, n)
            ts, ws = mid_t.at[m, u], mid_w.at[m, u]
        value = chain(ts[1], ts[0]) if n == 0 else chain(ts[1], ws[0]) + ws[1]
        if m + 1 < n_mid:
            (mid_t, mid_w)[n][m + 1, u, bit_of(middle[m + 1])] = value
            send_mid(m + 1, u, n)
        else:
            (top_t, top_w)[n][u, mine] = value
            send_top(u, n)

    def reads(group):
        for j in group:
            q_copy(j).wait_recv()
        for j in group:
            h = core * slots + j
            for e in range(2):
                if e == 0:
                    qb, kb = q_ref[:, columns(h)], k_ref[:, columns(h)]
                else:
                    qb, kb = q_in[j].astype(BF16), kv_in[j, :size].astype(BF16)
                s = other if e else core
                r, inside = local_reads(qb, kb, pairs[e, j], colb[e, j], gains[e, j, :1])
                r_out[j, s, :size] = r
                r_out[j, s, size:] = (kv_in[j, 2 * size :] if e else aux[h])[4 : 4 + ROWS]
                near[j, s] = inside
        for j in group:
            seen = mm(split(r_out[j, 1, :size]), beside(turns[0, j], writes[0, j]))
            weight = jnp.where(core == 1, colb[0, j], colb[1, j])[:, 3:4]
            r_out[j, 1, :size] = seen[:, :dim]
            near[j, 1] += weight * seen[:, dim:]

    r_copies = {}

    def send_reads(u):
        j = 2 * u + 1 - zl
        for s in range(2):
            i = 2 * u + s
            r_copies[u, s] = begin(
                remote(r_out.at[j, s], r_in.at[u, zl, s], s_r.at[i], r_r.at[i], across)
            )
            r_in[u, zl, s] = r_out[2 * u + zl, s]

    def read(u, items, lower, l, fresh=False):
        rows = jnp.concatenate([r_in[u, z, s, :size] for z, s in items], 0)
        seen = mm(split(rows), lower)
        for n, (z, s) in enumerate(items):
            part = seen[n * size : (n + 1) * size]
            value = colr[u, z, s][:, l - 1 : l] * part[:, dim:]
            far[u, z, s] = value if fresh else far[u, z, s] + value
            r_in[u, z, s, :size] = part[:, :dim]

    everyone = [(z, s) for z in range(2) for s in range(2)]

    def low_reads(u):
        for s in range(2):
            r_copies[u, s].wait_recv()
        for z, s in everyone:
            colr[u, z, s] = r_in[u, z, s, size:].T
        for s in range(2):
            far[u, 0, s] = jnp.zeros((size, dim), F32)
        read(u, everyone[2:], beside(low_t[u, 0], low_w[u, 0]), 1, fresh=True)

    def mid_reads(u):
        for m, l in enumerate(middle):

            @pl.when(bit_of(l) == 1)
            def _():
                read(u, everyone, beside(mid_t[m, u, 0], mid_w[m, u, 0]), l)

    def far_copy(u, n):
        z, s, device = (
            (1 - zl, core, across),
            (1 - zl, other, diagonal),
            (zl, other, beside_me),
        )[n]
        h = core * slots + 2 * u + zl
        i = 3 * u + n
        return remote(far.at[u, z, s], far_in.at[h], s_far.at[i], r_far.at[i], device)

    def top_reads(u):
        @pl.when(second_x)
        def _():
            wait_top(u, 1, 0)
            pl.when(second_y)(functools.partial(wait_top, u, 0, 0))
            read(u, everyone, beside(top_t[u, 2 * yy], top_w[u, 2 * yy]), xl)

        @pl.when(second_y)
        def _():
            pl.when(second_x)(functools.partial(wait_top, u, 0, 1))
            pl.when(first_x)(functools.partial(wait_top, u, 0, 2))
            wait_top(u, 1, 1)
            wait_top(u, 1, 2)
            lower = split(chain(top_t[u, 1], top_w[u, 0]) + top_w[u, 1])
            for n, (z, s) in enumerate(
                ((1 - zl, core), (1 - zl, other), (zl, other), (zl, core))
            ):
                seen = mm(split(r_in[u, z, s, :size]), lower)
                far[u, z, s] += colr[u, z, s][:, yl - 1 : yl] * seen
                if n < 3:
                    far_copy(u, n).start()

        @pl.when(first_y)
        def _():
            for n in range(3):
                far_copy(u, n).start()

        far_in[core * slots + 2 * u + zl] = far[u, zl, core]

    solve([(j, 0) for j in away])
    loads[0].wait()
    for j in range(slots):
        q_out[j] = q_ref[:, columns(other * slots + j)].astype(F32)
    for j in range(slots):
        begin(q_copy(j))
    for j in away:
        kv_copy(j).wait_recv()
    solve([(j, 1) for j in away])
    for u in range(waves):
        merge(away[u])
    for n in range(2):
        node_copies[0][n].start()
    for n in range(2):
        node_copies[1][n].start()
    for j in kept:
        kv_copy(j).wait_recv()
    solve([(j, e) for j in kept for e in range(2)])
    for u in range(waves):
        merge(kept[u])
        low_t[u, zl] = node_t[kept[u]]
        low_w[u, zl] = node_w[kept[u]]
    lift(-1, 0, 0)
    lift(-1, 0, 1)
    reads((0, 1))
    reads((2, 3))
    send_reads(0)
    near_copies = [
        begin(
            remote(near.at[j, other], near_in.at[j], s_near.at[j], r_near.at[j], beside_me)
        )
        for j in range(slots)
    ]
    for m in range(n_mid - 1):
        lift(m, 0, 0)
        lift(m, 0, 1)
    lift(n_mid - 1, 0, 0)
    lift(-1, 1, 0)
    lift(-1, 1, 1)
    send_reads(1)
    lift(n_mid - 1, 0, 1)
    for m in range(n_mid - 1):
        lift(m, 1, 0)
        lift(m, 1, 1)
    lift(n_mid - 1, 1, 0)
    lift(n_mid - 1, 1, 1)
    for u in range(waves):
        low_reads(u)
        mid_reads(u)
        top_reads(u)

    for copy in near_copies:
        copy.wait_recv()
    for u in range(waves):
        for n, (c, z) in enumerate(((core, 1 - zl), (other, 1 - zl), (other, zl), (core, zl))):
            j = 2 * u + z
            h = c * slots + j
            if n < 3:
                i = 3 * u + n
                device = (across, diagonal, beside_me)[n]
                remote(
                    far.at[u, zl, core], far_in.at[h], s_far.at[i], r_far.at[i], device
                ).wait_recv()
            here = near[j, core] if n in (0, 3) else near_in[j]
            out_ref[:, columns(h)] = here + far_in[h]
    for copy in pending:
        copy.wait_send()
    for u in range(waves):
        for n in range(3):
            far_copy(u, n).wait_send()
        for n in range(2):
            each_top(u, n, lambda copy: copy.wait_send())


def on_device(n_grp, n_seq, queries, keys, values, forget, beta, level_weights):
    size = queries.shape[0]
    heads = forget.shape[1]
    dim = queries.shape[1] // heads
    slots = heads // 2
    n_mid = (n_grp * n_seq).bit_length() - 5
    dma = pltpu.SemaphoreType.DMA
    small = forget.T, beta.T, jnp.transpose(level_weights, (0, 2, 1))
    arguments = (queries, keys, values, *small)

    def vmem(*shape):
        return pltpu.VMEM(shape, F32)

    return pl.pallas_call(
        functools.partial(kernel, n_grp, n_seq, heads),
        out_shape=pltpu.VMEM((size, heads * dim), F32),
        in_specs=[pl.BlockSpec(memory_space=pl.ANY)] * 6,
        out_specs=pl.BlockSpec(memory_space=pltpu.VMEM),
        scratch_shapes=[
            vmem(heads, AUX, size),
            vmem(slots, 2 * size + AUX, dim),
            vmem(slots, size, dim),
            vmem(slots, 2 * size + AUX, dim),
            vmem(slots, size, dim),
            vmem(2, slots, size, 2 * dim),
            vmem(2, slots, size, AUX),
            vmem(2, slots, 8, size),
        ]
        + [vmem(2, slots, dim, dim)] * 2
        + [vmem(slots, dim, dim)] * 2
        + [vmem(2, 2, dim, dim)] * 2
        + [
            vmem(slots, 2, size + ROWS, dim),
            vmem(2, 2, 2, size + ROWS, dim),
            vmem(2, 2, 2, size, ROWS),
            vmem(slots, 2, size, dim),
            vmem(slots, size, dim),
            vmem(2, 2, 2, size, dim),
            vmem(heads, size, dim),
        ]
        + [vmem(n_mid, 2, 2, dim, dim)] * 2
        + [vmem(2, 4, dim, dim)] * 2
        + [pltpu.VMEM(a.shape, a.dtype) for a in arguments]
        + [dma((slots,))] * 4
        + [dma((4,))] * 4
        + [dma((n_mid, 4))] * 2
        + [dma((12,))] * 2
        + [dma((slots,))] * 2
        + [dma((6,))] * 3,
        compiler_params=pltpu.CompilerParams(collective_id=0, has_side_effects=True),
    )(*arguments)


def solution(mesh):
    both = P(("grp", "seq"), None)
    return jax.shard_map(
        functools.partial(on_device, mesh.shape["grp"], mesh.shape["seq"]),
        mesh=mesh,
        in_specs=(both, both, both, both, both, P(None, ("grp", "seq"), None)),
        out_specs=both,
        check_vma=False,
    )
```

```python
import functools

import jax
import jax.numpy as jnp
from jax import lax
from jax.experimental import pallas as pl
from jax.experimental.pallas import tpu as pltpu
from jax.sharding import PartitionSpec as P

MESH = pl.DeviceIdType.MESH
F32 = jnp.float32
BF16 = jnp.bfloat16
NN = (((1,), (0,)), ((), ()))
NT = (((1,), (1,)), ((), ()))
AUX = 16
ROWS = 8
TILE = 16
EPS = 1e-06


def dot(a, b, dims=NN):
    return lax.dot_general(a, b, dims, preferred_element_type=F32)


def split(a):
    high = a.astype(BF16)
    return high, (a - high.astype(F32)).astype(BF16)


def mm(a, b):
    ah, al = a
    bh, bl = b
    return dot(ah, bh) + (dot(ah, bl) + dot(al, bh))


def mm_square(a, b):
    ah, al = a
    bh, bl = b
    right = jnp.concatenate(
        [jnp.concatenate([bh, bl], 1), jnp.concatenate([bh, jnp.zeros_like(bl)], 1)], 0
    )
    both = dot(jnp.concatenate([ah, al], 1), right)
    width = bh.shape[1]
    return both[:, :width] + both[:, width:]


def mm_exact(a, b):
    return dot(jnp.concatenate(a, 1), jnp.concatenate([b, b], 0))


def tile_inverse(low, size):
    lane = lax.broadcasted_iota(jnp.int32, (TILE, size), 1)
    sub = lax.broadcasted_iota(jnp.int32, (TILE, size), 0)
    tile = lane // TILE
    packed = low[:TILE]
    for g in range(1, size // TILE):
        packed = jnp.where(tile == g, low[g * TILE : (g + 1) * TILE], packed)
    inner = lane - tile * TILE
    packed = jnp.where(sub > inner, packed, 0.0)
    x = jnp.where(sub == inner, 1.0, 0.0)
    for c in range(TILE - 1):
        column = jnp.take_along_axis(packed, tile * TILE + c, axis=1)
        x = x - column * x[c : c + 1]
    return jnp.concatenate(
        [jnp.where(tile == g, x, 0.0) for g in range(size // TILE)], 0
    )


def unit_lower_inverse(lowers, size, row, col):
    apart = row ^ col
    inverses = [tile_inverse(low, size) for low in lowers]
    width = TILE
    while width < size:
        mask = (apart >= width) & (apart < 2 * width)
        parts = [split(x) for x in inverses]
        blocks = [split(jnp.where(mask, low, 0.0)) for low in lowers]
        left = [split(mm_square(x, b)) for x, b in zip(parts, blocks)]
        inverses = [x - mm_square(l, p) for x, l, p in zip(inverses, left, parts)]
        width *= 2
    return inverses


def transitions(blocks, size, dim):
    row = lax.broadcasted_iota(jnp.int32, (size, size), 0)
    col = lax.broadcasted_iota(jnp.int32, (size, size), 1)
    aux_row = lax.broadcasted_iota(jnp.int32, (AUX, size), 0)
    staged, lowers = [], []
    for kb, vb, aux in blocks:
        gram = dot(kb, kb, NT)
        norm = jnp.sum(jnp.where(row == col, gram, 0.0), 0, keepdims=True) + EPS
        rk = lax.rsqrt(norm)
        gain = aux[1:2] * (rk * rk)
        decay = aux[0:1]
        cols = jnp.where(aux_row == AUX - 1, gain, aux).T
        lowers.append(jnp.where(row > col, gram * gain, 0.0))
        staged.append((kb, vb, gain, norm * rk / decay, decay[:, size - 1 : size], cols))
    inverses = unit_lower_inverse(lowers, size, row, col)
    eye = (row == col).astype(F32)
    results = []
    for inverse, (kb, vb, gain, unscale, last, cols) in zip(inverses, staged):
        y = mm_exact(split(inverse), kb)
        z = mm_exact(split(inverse * unscale), vb)
        pair = jnp.concatenate([y, z], 1)
        kt = kb.astype(F32).T.astype(BF16)
        moved = dot(
            jnp.concatenate([kt, kt], 1),
            jnp.concatenate(split(pair * cols[:, AUX - 1 : AUX]), 0),
        )
        turn, write = last * (eye - moved[:, :dim]), last * moved[:, dim:]
        results.append((turn, write, pair, cols, gain))
    return results


def local_reads(qb, kb, pair, cols, gain):
    size = qb.shape[0]
    dim = qb.shape[1]
    row = lax.broadcasted_iota(jnp.int32, (size, size), 0)
    col = lax.broadcasted_iota(jnp.int32, (size, size), 1)
    q = qb.astype(F32)
    scale = lax.rsqrt(jnp.sum(q * q, -1, keepdims=True) + EPS) * cols[:, 0:1]
    scores = jnp.where(row >= col, dot(qb, kb, NT) * gain, 0.0)
    seen = mm(split(scores), split(pair))
    return scale * (q - seen[:, :dim]), (scale * cols[:, 2:3]) * seen[:, dim:]


def chain(upper, lower):
    return mm_square(split(upper), split(lower))


def beside(turn, write):
    th, tl = split(turn)
    wh, wl = split(write)
    return jnp.concatenate([th, wh], 1), jnp.concatenate([tl, wl], 1)


def kernel(n_grp, n_seq, heads, *refs):
    arguments, out_ref = refs[:6], refs[6]
    (
        aux,
        kv_out,
        q_out,
        kv_in,
        q_in,
        pairs,
        colb,
        gains,
        turns,
        writes,
        node_t,
        node_w,
        low_t,
        low_w,
        r_out,
        r_in,
        colr,
        near,
        near_in,
        far,
        far_in,
        mid_t,
        mid_w,
        top_t,
        top_w,
        *held,
    ) = refs[7:38]
    q_ref, k_ref, v_ref, f_ref, b_ref, w_ref = held
    (
        s_kv,
        r_kv,
        s_q,
        r_q,
        s_node,
        r_node,
        s_r,
        r_r,
        s_mid,
        r_mid,
        s_top,
        r_top,
        s_near,
        r_near,
        s_far,
        r_far,
        s_load,
    ) = refs[38:]
    total_bits = (n_grp * n_seq).bit_length() - 1
    middle = list(range(2, total_bits - 2))
    xl, yl = total_bits - 2, total_bits - 1
    n_mid = len(middle)
    size = q_ref.shape[0]
    dim = q_ref.shape[1] // heads
    slots = heads // 2
    waves = slots // 2
    pos = lax.axis_index("grp") * n_seq + lax.axis_index("seq")

    def bit_of(l):
        return (pos // (1 << l)) % 2

    def where_is(number):
        return (number // n_seq, number % n_seq)

    def flipped(*ls):
        return where_is(pos + sum((1 - 2 * bit_of(l)) * (1 << l) for l in ls))

    def columns(i):
        return pl.ds(pl.multiple_of(i * dim, dim), dim)

    def remote(source, target, send, receive, device):
        return pltpu.make_async_remote_copy(
            src_ref=source,
            dst_ref=target,
            send_sem=send,
            recv_sem=receive,
            device_id=device,
            device_id_type=MESH,
        )

    core, zl, xx, yy = bit_of(0), bit_of(1), bit_of(xl), bit_of(yl)
    other = 1 - core
    beside_me, across, diagonal = flipped(0), flipped(1), flipped(0, 1)
    tops = (flipped(xl), flipped(yl), flipped(xl, yl))
    mine = 2 * yy + xx
    theirs = (2 * yy + 1 - xx, 2 * (1 - yy) + xx, 2 * (1 - yy) + 1 - xx)
    greeted = [beside_me, across, diagonal, *tops] + [flipped(l) for l in middle]
    barrier = pltpu.get_barrier_semaphore()
    for device in greeted:
        pl.semaphore_signal(barrier, inc=1, device_id=device, device_id_type=MESH)

    loads = [
        pltpu.make_async_copy(source, target, s_load.at[i])
        for i, (source, target) in enumerate(zip(arguments, held))
    ]
    for i in (3, 4, 5, 1, 2, 0):
        loads[i].start()
    for i in (3, 4, 5):
        loads[i].wait()

    total = f_ref[...]
    lane = lax.broadcasted_iota(jnp.int32, total.shape, 1)
    step = 1
    while step < size:
        total = total + jnp.where(lane >= step, pltpu.roll(total, step, 1), 0.0)
        step *= 2
    decay = jnp.exp(-total)
    aux[...] = jnp.zeros_like(aux)
    levels = w_ref.shape[0]
    for h in range(heads):
        aux[h, 0:1] = decay[h : h + 1]
        aux[h, 1:2] = b_ref[h : h + 1]
        for l in range(levels):
            aux[h, 2 + l : 3 + l] = w_ref[l, h : h + 1]

    away = [2 * u + 1 - zl for u in range(waves)]
    kept = [2 * u + zl for u in range(waves)]
    loads[1].wait()
    loads[2].wait()
    for j in away + kept:
        h = other * slots + j
        kv_out[j, :size] = k_ref[:, columns(h)].astype(F32)
        kv_out[j, size : 2 * size] = v_ref[:, columns(h)].astype(F32)
        kv_out[j, 2 * size :] = aux[h]
    pl.semaphore_wait(barrier, len(greeted))

    pending = []

    def begin(copy):
        copy.start()
        pending.append(copy)
        return copy

    def kv_copy(j):
        return remote(kv_out.at[j], kv_in.at[j], s_kv.at[j], r_kv.at[j], beside_me)

    def q_copy(j):
        return remote(q_out.at[j], q_in.at[j], s_q.at[j], r_q.at[j], beside_me)

    for j in away + kept:
        begin(kv_copy(j))

    def own_block(j):
        h = core * slots + j
        return k_ref[:, columns(h)], v_ref[:, columns(h)], aux[h]

    def other_block(j):
        return (
            kv_in[j, :size].astype(BF16),
            kv_in[j, size : 2 * size].astype(BF16),
            kv_in[j, 2 * size :],
        )

    def solve(work):
        done = transitions(
            [own_block(j) if e == 0 else other_block(j) for j, e in work], size, dim
        )
        for (j, e), (turn, write, pair, cols, gain) in zip(work, done):
            s = other if e else core
            turns[s, j] = turn
            writes[s, j] = write
            pairs[e, j] = pair
            colb[e, j] = cols
            gains[e, j] = jnp.broadcast_to(gain, (8, size))

    node_copies = [
        [
            remote(
                source.at[2 * u + 1 - zl],
                target.at[u, zl],
                s_node.at[2 * u + n],
                r_node.at[2 * u + n],
                across,
            )
            for n, (source, target) in enumerate(((node_t, low_t), (node_w, low_w)))
        ]
        for u in range(waves)
    ]
    pending += [copy for copies in node_copies for copy in copies]

    def send_nodes(u):
        for copy in node_copies[u]:
            copy.start()

    def merge(j):
        upper = turns[1, j]
        node_t[j] = chain(upper, turns[0, j])
        node_w[j] = chain(upper, writes[0, j]) + writes[1, j]

    def send_mid(m, u, n):
        l = middle[m]
        ref = (mid_t, mid_w)[n].at[m, u, bit_of(l)]
        begin(remote(ref, ref, s_mid.at[m, 2 * u + n], r_mid.at[m, 2 * u + n], flipped(l)))

    def wait_mid(m, u, n):
        l = middle[m]
        ref = (mid_t, mid_w)[n].at[m, u, 1 - bit_of(l)]
        remote(
            ref, ref, s_mid.at[m, 2 * u + n], r_mid.at[m, 2 * u + n], flipped(l)
        ).wait_recv()

    first_x, second_x = xx == 0, xx == 1
    first_y, second_y = yy == 0, yy == 1

    def top_copy(u, n, p, group):
        ref = (top_t, top_w)[n].at[u, group]
        i = 4 * p + 2 * u + n
        return remote(ref, ref, s_top.at[i], r_top.at[i], tops[p])

    def each_top(u, n, act):
        def do(*ps):
            def run():
                for p in ps:
                    act(top_copy(u, n, p, mine))

            return run

        if n == 1:
            pl.when(first_x)(do(0))
            pl.when(first_y)(do(1, 2))
        else:
            pl.when(first_x & second_y)(do(0))
            pl.when(second_x & first_y)(do(1, 2))

    def send_top(u, n):
        each_top(u, n, lambda copy: copy.start())

    def wait_top(u, n, p):
        top_copy(u, n, p, theirs[p]).wait_recv()

    def lift(m, u, n):
        if m < 0:
            node_copies[u][n].wait_recv()
            ts, ws = low_t.at[u], low_w.at[u]
        else:
            wait_mid(m, u, n)
            ts, ws = mid_t.at[m, u], mid_w.at[m, u]
        value = chain(ts[1], ts[0]) if n == 0 else chain(ts[1], ws[0]) + ws[1]
        if m + 1 < n_mid:
            (mid_t, mid_w)[n][m + 1, u, bit_of(middle[m + 1])] = value
            send_mid(m + 1, u, n)
        else:
            (top_t, top_w)[n][u, mine] = value
            send_top(u, n)

    def reads(group):
        for j in group:
            q_copy(j).wait_recv()
        for j in group:
            h = core * slots + j
            for e in range(2):
                if e == 0:
                    qb, kb = q_ref[:, columns(h)], k_ref[:, columns(h)]
                else:
                    qb, kb = q_in[j].astype(BF16), kv_in[j, :size].astype(BF16)
                s = other if e else core
                r, inside = local_reads(qb, kb, pairs[e, j], colb[e, j], gains[e, j, :1])
                r_out[j, s, :size] = r
                r_out[j, s, size:] = (kv_in[j, 2 * size :] if e else aux[h])[4 : 4 + ROWS]
                near[j, s] = inside
        for j in group:
            seen = mm(split(r_out[j, 1, :size]), beside(turns[0, j], writes[0, j]))
            weight = jnp.where(core == 1, colb[0, j], colb[1, j])[:, 3:4]
            r_out[j, 1, :size] = seen[:, :dim]
            near[j, 1] += weight * seen[:, dim:]

    r_copies = {}

    def send_reads(u):
        j = 2 * u + 1 - zl
        for s in range(2):
            i = 2 * u + s
            r_copies[u, s] = begin(
                remote(r_out.at[j, s], r_in.at[u, zl, s], s_r.at[i], r_r.at[i], across)
            )

    def keep_reads():
        for u in range(waves):
            for s in range(2):
                r_in[u, zl, s] = r_out[kept[u], s]

    def read(u, items, lower, l, fresh=False):
        rows = jnp.concatenate([r_in[u, z, s, :size] for z, s in items], 0)
        seen = mm(split(rows), lower)
        for n, (z, s) in enumerate(items):
            part = seen[n * size : (n + 1) * size]
            value = colr[u, z, s][:, l - 1 : l] * part[:, dim:]
            far[u, z, s] = value if fresh else far[u, z, s] + value
            r_in[u, z, s, :size] = part[:, :dim]

    everyone = [(z, s) for z in range(2) for s in range(2)]

    def low_reads(u):
        for s in range(2):
            r_copies[u, s].wait_recv()
        for z, s in everyone:
            colr[u, z, s] = r_in[u, z, s, size:].T
        for s in range(2):
            far[u, 0, s] = jnp.zeros((size, dim), F32)
        read(u, everyone[2:], beside(low_t[u, 0], low_w[u, 0]), 1, fresh=True)

    def mid_reads(u):
        for m, l in enumerate(middle):

            @pl.when(bit_of(l) == 1)
            def _():
                read(u, everyone, beside(mid_t[m, u, 0], mid_w[m, u, 0]), l)

    def far_copy(u, n):
        z, s, device = (
            (1 - zl, core, across),
            (1 - zl, other, diagonal),
            (zl, other, beside_me),
        )[n]
        h = core * slots + 2 * u + zl
        i = 3 * u + n
        return remote(far.at[u, z, s], far_in.at[h], s_far.at[i], r_far.at[i], device)

    def top_reads(u):
        @pl.when(second_x)
        def _():
            wait_top(u, 1, 0)
            pl.when(second_y)(functools.partial(wait_top, u, 0, 0))
            read(u, everyone, beside(top_t[u, 2 * yy], top_w[u, 2 * yy]), xl)

        @pl.when(second_y)
        def _():
            pl.when(second_x)(functools.partial(wait_top, u, 0, 1))
            pl.when(first_x)(functools.partial(wait_top, u, 0, 2))
            wait_top(u, 1, 1)
            wait_top(u, 1, 2)
            lower = split(chain(top_t[u, 1], top_w[u, 0]) + top_w[u, 1])
            for n, (z, s) in enumerate(
                ((1 - zl, core), (1 - zl, other), (zl, other), (zl, core))
            ):
                seen = mm(split(r_in[u, z, s, :size]), lower)
                far[u, z, s] += colr[u, z, s][:, yl - 1 : yl] * seen
                if n < 3:
                    far_copy(u, n).start()

        @pl.when(first_y)
        def _():
            for n in range(3):
                far_copy(u, n).start()

        far_in[core * slots + 2 * u + zl] = far[u, zl, core]

    solve([(j, 0) for j in away])
    loads[0].wait()
    for j in range(slots):
        q_out[j] = q_ref[:, columns(other * slots + j)].astype(F32)
    for j in range(slots):
        begin(q_copy(j))
    for j in away:
        kv_copy(j).wait_recv()
    solve([(j, 1) for j in away])
    for u in range(waves):
        merge(away[u])
    for n in range(2):
        node_copies[0][n].start()
    for n in range(2):
        node_copies[1][n].start()
    for j in kept:
        kv_copy(j).wait_recv()
    solve([(j, e) for j in kept for e in range(2)])
    for u in range(waves):
        merge(kept[u])
        low_t[u, zl] = node_t[kept[u]]
        low_w[u, zl] = node_w[kept[u]]
    lift(-1, 0, 0)
    lift(-1, 0, 1)
    reads(away)
    send_reads(0)
    for m in range(n_mid - 1):
        lift(m, 0, 0)
        lift(m, 0, 1)
    lift(n_mid - 1, 0, 0)
    lift(-1, 1, 0)
    lift(-1, 1, 1)
    send_reads(1)
    reads(kept)
    keep_reads()
    near_copies = [
        begin(
            remote(near.at[j, other], near_in.at[j], s_near.at[j], r_near.at[j], beside_me)
        )
        for j in range(slots)
    ]
    lift(n_mid - 1, 0, 1)
    for m in range(n_mid - 1):
        lift(m, 1, 0)
        lift(m, 1, 1)
    lift(n_mid - 1, 1, 0)
    lift(n_mid - 1, 1, 1)
    for u in range(waves):
        low_reads(u)
        mid_reads(u)
        top_reads(u)

    for u in range(waves):
        for n in range(2):
            each_top(u, n, lambda copy: copy.wait_send())
    for copy in pending:
        copy.wait_send()
    for copy in near_copies:
        copy.wait_recv()
    for u in range(waves):
        for n, (c, z) in enumerate(((core, 1 - zl), (other, 1 - zl), (other, zl), (core, zl))):
            j = 2 * u + z
            h = c * slots + j
            if n < 3:
                i = 3 * u + n
                device = (across, diagonal, beside_me)[n]
                remote(
                    far.at[u, zl, core], far_in.at[h], s_far.at[i], r_far.at[i], device
                ).wait_recv()
            here = near[j, core] if n in (0, 3) else near_in[j]
            out_ref[:, columns(h)] = here + far_in[h]
    for u in range(waves):
        for n in range(3):
            far_copy(u, n).wait_send()


def on_device(n_grp, n_seq, queries, keys, values, forget, beta, level_weights):
    size = queries.shape[0]
    heads = forget.shape[1]
    dim = queries.shape[1] // heads
    slots = heads // 2
    n_mid = (n_grp * n_seq).bit_length() - 5
    dma = pltpu.SemaphoreType.DMA
    small = forget.T, beta.T, jnp.transpose(level_weights, (0, 2, 1))
    arguments = (queries, keys, values, *small)

    def vmem(*shape):
        return pltpu.VMEM(shape, F32)

    return pl.pallas_call(
        functools.partial(kernel, n_grp, n_seq, heads),
        out_shape=pltpu.VMEM((size, heads * dim), F32),
        in_specs=[pl.BlockSpec(memory_space=pl.ANY)] * 6,
        out_specs=pl.BlockSpec(memory_space=pltpu.VMEM),
        scratch_shapes=[
            vmem(heads, AUX, size),
            vmem(slots, 2 * size + AUX, dim),
            vmem(slots, size, dim),
            vmem(slots, 2 * size + AUX, dim),
            vmem(slots, size, dim),
            vmem(2, slots, size, 2 * dim),
            vmem(2, slots, size, AUX),
            vmem(2, slots, 8, size),
        ]
        + [vmem(2, slots, dim, dim)] * 2
        + [vmem(slots, dim, dim)] * 2
        + [vmem(2, 2, dim, dim)] * 2
        + [
            vmem(slots, 2, size + ROWS, dim),
            vmem(2, 2, 2, size + ROWS, dim),
            vmem(2, 2, 2, size, ROWS),
            vmem(slots, 2, size, dim),
            vmem(slots, size, dim),
            vmem(2, 2, 2, size, dim),
            vmem(heads, size, dim),
        ]
        + [vmem(n_mid, 2, 2, dim, dim)] * 2
        + [vmem(2, 4, dim, dim)] * 2
        + [pltpu.VMEM(a.shape, a.dtype) for a in arguments]
        + [dma((slots,))] * 4
        + [dma((4,))] * 4
        + [dma((n_mid, 4))] * 2
        + [dma((12,))] * 2
        + [dma((slots,))] * 2
        + [dma((6,))] * 3,
        compiler_params=pltpu.CompilerParams(collective_id=0, has_side_effects=True),
    )(*arguments)


def solution(mesh):
    both = P(("grp", "seq"), None)
    return jax.shard_map(
        functools.partial(on_device, mesh.shape["grp"], mesh.shape["seq"]),
        mesh=mesh,
        in_specs=(both, both, both, both, both, P(None, ("grp", "seq"), None)),
        out_specs=both,
        check_vma=False,
    )
```

```python
import functools

import jax
import jax.numpy as jnp
from jax import lax
from jax.experimental import pallas as pl
from jax.experimental.pallas import tpu as pltpu
from jax.sharding import PartitionSpec as P

MESH = pl.DeviceIdType.MESH
F32 = jnp.float32
BF16 = jnp.bfloat16
NN = (((1,), (0,)), ((), ()))
NT = (((1,), (1,)), ((), ()))
AUX = 16
ROWS = 8
TILE = 16
EPS = 1e-06


def dot(a, b, dims=NN):
    return lax.dot_general(a, b, dims, preferred_element_type=F32)


def split(a):
    high = a.astype(BF16)
    return high, (a - high.astype(F32)).astype(BF16)


def mm(a, b):
    ah, al = a
    bh, bl = b
    return dot(ah, bh) + (dot(ah, bl) + dot(al, bh))


def mm_square(a, b):
    ah, al = a
    bh, bl = b
    right = jnp.concatenate(
        [jnp.concatenate([bh, bl], 1), jnp.concatenate([bh, jnp.zeros_like(bl)], 1)], 0
    )
    both = dot(jnp.concatenate([ah, al], 1), right)
    width = bh.shape[1]
    return both[:, :width] + both[:, width:]


def mm_exact(a, b):
    return dot(jnp.concatenate(a, 1), jnp.concatenate([b, b], 0))


def tile_inverse(low, size):
    lane = lax.broadcasted_iota(jnp.int32, (TILE, size), 1)
    sub = lax.broadcasted_iota(jnp.int32, (TILE, size), 0)
    tile = lane // TILE
    packed = low[:TILE]
    for g in range(1, size // TILE):
        packed = jnp.where(tile == g, low[g * TILE : (g + 1) * TILE], packed)
    inner = lane - tile * TILE
    packed = jnp.where(sub > inner, packed, 0.0)
    x = jnp.where(sub == inner, 1.0, 0.0)
    for c in range(TILE - 1):
        column = jnp.take_along_axis(packed, tile * TILE + c, axis=1)
        x = x - column * x[c : c + 1]
    return jnp.concatenate(
        [jnp.where(tile == g, x, 0.0) for g in range(size // TILE)], 0
    )


def unit_lower_inverse(lowers, size, row, col):
    apart = row ^ col
    inverses = [tile_inverse(low, size) for low in lowers]
    width = TILE
    while width < size:
        mask = (apart >= width) & (apart < 2 * width)
        parts = [split(x) for x in inverses]
        blocks = [split(jnp.where(mask, low, 0.0)) for low in lowers]
        left = [split(mm_square(x, b)) for x, b in zip(parts, blocks)]
        inverses = [x - mm_square(l, p) for x, l, p in zip(inverses, left, parts)]
        width *= 2
    return inverses


def transitions(blocks, size, dim):
    row = lax.broadcasted_iota(jnp.int32, (size, size), 0)
    col = lax.broadcasted_iota(jnp.int32, (size, size), 1)
    aux_row = lax.broadcasted_iota(jnp.int32, (AUX, size), 0)
    staged, lowers = [], []
    for kb, vb, aux in blocks:
        gram = dot(kb, kb, NT)
        norm = jnp.sum(jnp.where(row == col, gram, 0.0), 0, keepdims=True) + EPS
        rk = lax.rsqrt(norm)
        gain = aux[1:2] * (rk * rk)
        decay = aux[0:1]
        cols = jnp.where(aux_row == AUX - 1, gain, aux).T
        lowers.append(jnp.where(row > col, gram * gain, 0.0))
        staged.append((kb, vb, gain, norm * rk / decay, decay[:, size - 1 : size], cols))
    inverses = unit_lower_inverse(lowers, size, row, col)
    eye = (row == col).astype(F32)
    results = []
    for inverse, (kb, vb, gain, unscale, last, cols) in zip(inverses, staged):
        y = mm_exact(split(inverse), kb)
        z = mm_exact(split(inverse * unscale), vb)
        pair = jnp.concatenate([y, z], 1)
        kt = kb.astype(F32).T.astype(BF16)
        moved = dot(
            jnp.concatenate([kt, kt], 1),
            jnp.concatenate(split(pair * cols[:, AUX - 1 : AUX]), 0),
        )
        turn, write = last * (eye - moved[:, :dim]), last * moved[:, dim:]
        results.append((turn, write, pair, cols, gain))
    return results


def local_reads(qb, kb, pair, cols, gain):
    size = qb.shape[0]
    dim = qb.shape[1]
    row = lax.broadcasted_iota(jnp.int32, (size, size), 0)
    col = lax.broadcasted_iota(jnp.int32, (size, size), 1)
    q = qb.astype(F32)
    scale = lax.rsqrt(jnp.sum(q * q, -1, keepdims=True) + EPS) * cols[:, 0:1]
    scores = jnp.where(row >= col, dot(qb, kb, NT) * gain, 0.0)
    seen = mm(split(scores), split(pair))
    return scale * (q - seen[:, :dim]), (scale * cols[:, 2:3]) * seen[:, dim:]


def chain(upper, lower):
    return mm_square(split(upper), split(lower))


def beside(turn, write):
    th, tl = split(turn)
    wh, wl = split(write)
    return jnp.concatenate([th, wh], 1), jnp.concatenate([tl, wl], 1)


def kernel(n_grp, n_seq, heads, *refs):
    arguments, out_ref = refs[:6], refs[6]
    (
        aux,
        kv_out,
        q_out,
        kv_in,
        q_in,
        pairs,
        colb,
        gains,
        turns,
        writes,
        node_t,
        node_w,
        low_t,
        low_w,
        r_out,
        r_in,
        colr,
        near,
        near_in,
        far,
        far_in,
        mid_t,
        mid_w,
        top_t,
        top_w,
        *held,
    ) = refs[7:38]
    q_ref, k_ref, v_ref, f_ref, b_ref, w_ref = held
    (
        s_kv,
        r_kv,
        s_q,
        r_q,
        s_node,
        r_node,
        s_r,
        r_r,
        s_mid,
        r_mid,
        s_top,
        r_top,
        s_near,
        r_near,
        s_far,
        r_far,
        s_load,
    ) = refs[38:]
    total_bits = (n_grp * n_seq).bit_length() - 1
    middle = list(range(2, total_bits - 2))
    xl, yl = total_bits - 2, total_bits - 1
    n_mid = len(middle)
    size = q_ref.shape[0]
    dim = q_ref.shape[1] // heads
    slots = heads // 2
    waves = slots // 2
    pos = lax.axis_index("grp") * n_seq + lax.axis_index("seq")

    def bit_of(l):
        return (pos // (1 << l)) % 2

    def where_is(number):
        return (number // n_seq, number % n_seq)

    def flipped(*ls):
        return where_is(pos + sum((1 - 2 * bit_of(l)) * (1 << l) for l in ls))

    def columns(i):
        return pl.ds(pl.multiple_of(i * dim, dim), dim)

    def remote(source, target, send, receive, device):
        return pltpu.make_async_remote_copy(
            src_ref=source,
            dst_ref=target,
            send_sem=send,
            recv_sem=receive,
            device_id=device,
            device_id_type=MESH,
        )

    core, zl, xx, yy = bit_of(0), bit_of(1), bit_of(xl), bit_of(yl)
    other = 1 - core
    beside_me, across, diagonal = flipped(0), flipped(1), flipped(0, 1)
    tops = (flipped(xl), flipped(yl), flipped(xl, yl))
    mine = 2 * yy + xx
    theirs = (2 * yy + 1 - xx, 2 * (1 - yy) + xx, 2 * (1 - yy) + 1 - xx)
    greeted = [beside_me, across, diagonal, *tops] + [flipped(l) for l in middle]
    barrier = pltpu.get_barrier_semaphore()
    for device in greeted:
        pl.semaphore_signal(barrier, inc=1, device_id=device, device_id_type=MESH)

    loads = [
        pltpu.make_async_copy(source, target, s_load.at[i])
        for i, (source, target) in enumerate(zip(arguments, held))
    ]
    for i in (3, 4, 5, 1, 2, 0):
        loads[i].start()
    for i in (3, 4, 5):
        loads[i].wait()

    total = f_ref[...]
    lane = lax.broadcasted_iota(jnp.int32, total.shape, 1)
    step = 1
    while step < size:
        total = total + jnp.where(lane >= step, pltpu.roll(total, step, 1), 0.0)
        step *= 2
    decay = jnp.exp(-total)
    aux[...] = jnp.zeros_like(aux)
    levels = w_ref.shape[0]
    for h in range(heads):
        aux[h, 0:1] = decay[h : h + 1]
        aux[h, 1:2] = b_ref[h : h + 1]
        for l in range(levels):
            aux[h, 2 + l : 3 + l] = w_ref[l, h : h + 1]

    away = [2 * u + 1 - zl for u in range(waves)]
    kept = [2 * u + zl for u in range(waves)]
    loads[1].wait()
    loads[2].wait()
    for j in away + kept:
        h = other * slots + j
        kv_out[j, :size] = k_ref[:, columns(h)].astype(F32)
        kv_out[j, size : 2 * size] = v_ref[:, columns(h)].astype(F32)
        kv_out[j, 2 * size :] = aux[h]
    pl.semaphore_wait(barrier, len(greeted))

    pending = []

    def begin(copy):
        copy.start()
        pending.append(copy)
        return copy

    def kv_copy(j):
        return remote(kv_out.at[j], kv_in.at[j], s_kv.at[j], r_kv.at[j], beside_me)

    def q_copy(j):
        return remote(q_out.at[j], q_in.at[j], s_q.at[j], r_q.at[j], beside_me)

    for j in away + kept:
        begin(kv_copy(j))

    def own_block(j):
        h = core * slots + j
        return k_ref[:, columns(h)], v_ref[:, columns(h)], aux[h]

    def other_block(j):
        return (
            kv_in[j, :size].astype(BF16),
            kv_in[j, size : 2 * size].astype(BF16),
            kv_in[j, 2 * size :],
        )

    def solve(work):
        done = transitions(
            [own_block(j) if e == 0 else other_block(j) for j, e in work], size, dim
        )
        for (j, e), (turn, write, pair, cols, gain) in zip(work, done):
            s = other if e else core
            turns[s, j] = turn
            writes[s, j] = write
            pairs[e, j] = pair
            colb[e, j] = cols
            gains[e, j] = jnp.broadcast_to(gain, (8, size))

    late = []
    node_copies = [
        [
            remote(
                source.at[2 * u + 1 - zl],
                target.at[u, zl],
                s_node.at[2 * u + n],
                r_node.at[2 * u + n],
                across,
            )
            for n, (source, target) in enumerate(((node_t, low_t), (node_w, low_w)))
        ]
        for u in range(waves)
    ]
    pending += [copy for copies in node_copies for copy in copies]

    def send_nodes(u):
        for copy in node_copies[u]:
            copy.start()

    def merge(j):
        upper = turns[1, j]
        node_t[j] = chain(upper, turns[0, j])
        node_w[j] = chain(upper, writes[0, j]) + writes[1, j]

    def send_mid(m, u, n):
        l = middle[m]
        ref = (mid_t, mid_w)[n].at[m, u, bit_of(l)]
        copy = remote(ref, ref, s_mid.at[m, 2 * u + n], r_mid.at[m, 2 * u + n], flipped(l))
        if m + 1 < n_mid:
            begin(copy)
            return
        needed = first_x | first_y | (bit_of(l) == 0)
        pl.when(needed)(copy.start)
        late.append((needed, copy))

    def wait_mid(m, u, n):
        l = middle[m]
        ref = (mid_t, mid_w)[n].at[m, u, 1 - bit_of(l)]
        remote(
            ref, ref, s_mid.at[m, 2 * u + n], r_mid.at[m, 2 * u + n], flipped(l)
        ).wait_recv()

    first_x, second_x = xx == 0, xx == 1
    first_y, second_y = yy == 0, yy == 1

    def top_copy(u, n, p, group):
        ref = (top_t, top_w)[n].at[u, group]
        i = 4 * p + 2 * u + n
        return remote(ref, ref, s_top.at[i], r_top.at[i], tops[p])

    def each_top(u, n, act):
        def do(*ps):
            def run():
                for p in ps:
                    act(top_copy(u, n, p, mine))

            return run

        if n == 1:
            pl.when(first_x)(do(0))
            pl.when(first_y)(do(1, 2))
        else:
            pl.when(first_x & second_y)(do(0))
            pl.when(second_x & first_y)(do(1, 2))

    def send_top(u, n):
        each_top(u, n, lambda copy: copy.start())

    def wait_top(u, n, p):
        top_copy(u, n, p, theirs[p]).wait_recv()

    def lift(m, u, n):
        if m < 0:
            node_copies[u][n].wait_recv()
            ts, ws = low_t.at[u], low_w.at[u]
        else:
            ts, ws = mid_t.at[m, u], mid_w.at[m, u]

        def value():
            return chain(ts[1], ts[0]) if n == 0 else chain(ts[1], ws[0]) + ws[1]

        if m + 1 < n_mid:
            if m >= 0:
                wait_mid(m, u, n)
            (mid_t, mid_w)[n][m + 1, u, bit_of(middle[m + 1])] = value()
            send_mid(m + 1, u, n)
            return

        @pl.when(first_x | first_y)
        def _():
            wait_mid(m, u, n)
            (top_t, top_w)[n][u, mine] = value()
            send_top(u, n)

        @pl.when(second_x & second_y & (bit_of(middle[m]) == 1))
        def _():
            wait_mid(m, u, n)

    def reads(group):
        for j in group:
            q_copy(j).wait_recv()
        for j in group:
            h = core * slots + j
            for e in range(2):
                if e == 0:
                    qb, kb = q_ref[:, columns(h)], k_ref[:, columns(h)]
                else:
                    qb, kb = q_in[j].astype(BF16), kv_in[j, :size].astype(BF16)
                s = other if e else core
                r, inside = local_reads(qb, kb, pairs[e, j], colb[e, j], gains[e, j, :1])
                r_out[j, s, :size] = r
                r_out[j, s, size:] = (kv_in[j, 2 * size :] if e else aux[h])[4 : 4 + ROWS]
                near[j, s] = inside
        for j in group:
            seen = mm(split(r_out[j, 1, :size]), beside(turns[0, j], writes[0, j]))
            weight = jnp.where(core == 1, colb[0, j], colb[1, j])[:, 3:4]
            r_out[j, 1, :size] = seen[:, :dim]
            near[j, 1] += weight * seen[:, dim:]

    r_copies = {}

    def send_reads(u):
        j = 2 * u + 1 - zl
        for s in range(2):
            i = 2 * u + s
            r_copies[u, s] = begin(
                remote(r_out.at[j, s], r_in.at[u, zl, s], s_r.at[i], r_r.at[i], across)
            )

    def keep_reads():
        for u in range(waves):
            for s in range(2):
                r_in[u, zl, s] = r_out[kept[u], s]

    def read(u, items, lower, l, fresh=False):
        rows = jnp.concatenate([r_in[u, z, s, :size] for z, s in items], 0)
        seen = mm(split(rows), lower)
        for n, (z, s) in enumerate(items):
            part = seen[n * size : (n + 1) * size]
            value = colr[u, z, s][:, l - 1 : l] * part[:, dim:]
            far[u, z, s] = value if fresh else far[u, z, s] + value
            r_in[u, z, s, :size] = part[:, :dim]

    everyone = [(z, s) for z in range(2) for s in range(2)]

    def low_reads(u):
        for s in range(2):
            r_copies[u, s].wait_recv()
        for z, s in everyone:
            colr[u, z, s] = r_in[u, z, s, size:].T
        for s in range(2):
            far[u, 0, s] = jnp.zeros((size, dim), F32)
        read(u, everyone[2:], beside(low_t[u, 0], low_w[u, 0]), 1, fresh=True)

    def mid_reads(u):
        for m, l in enumerate(middle):

            @pl.when(bit_of(l) == 1)
            def _():
                read(u, everyone, beside(mid_t[m, u, 0], mid_w[m, u, 0]), l)

    def far_copy(u, n):
        z, s, device = (
            (1 - zl, core, across),
            (1 - zl, other, diagonal),
            (zl, other, beside_me),
        )[n]
        h = core * slots + 2 * u + zl
        i = 3 * u + n
        return remote(far.at[u, z, s], far_in.at[h], s_far.at[i], r_far.at[i], device)

    def top_reads(u):
        @pl.when(second_x)
        def _():
            wait_top(u, 1, 0)
            pl.when(second_y)(functools.partial(wait_top, u, 0, 0))
            read(u, everyone, beside(top_t[u, 2 * yy], top_w[u, 2 * yy]), xl)

        @pl.when(second_y)
        def _():
            pl.when(second_x)(functools.partial(wait_top, u, 0, 1))
            pl.when(first_x)(functools.partial(wait_top, u, 0, 2))
            wait_top(u, 1, 1)
            wait_top(u, 1, 2)
            lower = split(chain(top_t[u, 1], top_w[u, 0]) + top_w[u, 1])
            for n, (z, s) in enumerate(
                ((1 - zl, core), (1 - zl, other), (zl, other), (zl, core))
            ):
                seen = mm(split(r_in[u, z, s, :size]), lower)
                far[u, z, s] += colr[u, z, s][:, yl - 1 : yl] * seen
                if n < 3:
                    far_copy(u, n).start()

        @pl.when(first_y)
        def _():
            for n in range(3):
                far_copy(u, n).start()

        far_in[core * slots + 2 * u + zl] = far[u, zl, core]

    solve([(j, 0) for j in away])
    loads[0].wait()
    for j in range(slots):
        q_out[j] = q_ref[:, columns(other * slots + j)].astype(F32)
    for j in range(slots):
        begin(q_copy(j))
    for j in away:
        kv_copy(j).wait_recv()
    solve([(j, 1) for j in away])
    for u in range(waves):
        merge(away[u])
    for n in range(2):
        node_copies[0][n].start()
    for n in range(2):
        node_copies[1][n].start()
    for j in kept:
        kv_copy(j).wait_recv()
    solve([(j, e) for j in kept for e in range(2)])
    for u in range(waves):
        merge(kept[u])
        low_t[u, zl] = node_t[kept[u]]
        low_w[u, zl] = node_w[kept[u]]
    lift(-1, 0, 0)
    lift(-1, 0, 1)
    reads(away)
    send_reads(0)
    for m in range(n_mid - 1):
        lift(m, 0, 0)
        lift(m, 0, 1)
    lift(n_mid - 1, 0, 0)
    lift(-1, 1, 0)
    lift(-1, 1, 1)
    send_reads(1)
    reads(kept)
    keep_reads()
    near_copies = [
        begin(
            remote(near.at[j, other], near_in.at[j], s_near.at[j], r_near.at[j], beside_me)
        )
        for j in range(slots)
    ]
    lift(n_mid - 1, 0, 1)
    for m in range(n_mid - 1):
        lift(m, 1, 0)
        lift(m, 1, 1)
    lift(n_mid - 1, 1, 0)
    lift(n_mid - 1, 1, 1)
    for u in range(waves):
        low_reads(u)
        mid_reads(u)
        top_reads(u)

    for u in range(waves):
        for n in range(2):
            each_top(u, n, lambda copy: copy.wait_send())
    for copy in pending:
        copy.wait_send()
    for needed, copy in late:
        pl.when(needed)(copy.wait_send)
    for copy in near_copies:
        copy.wait_recv()
    for u in range(waves):
        for n, (c, z) in enumerate(((core, 1 - zl), (other, 1 - zl), (other, zl), (core, zl))):
            j = 2 * u + z
            h = c * slots + j
            if n < 3:
                i = 3 * u + n
                device = (across, diagonal, beside_me)[n]
                remote(
                    far.at[u, zl, core], far_in.at[h], s_far.at[i], r_far.at[i], device
                ).wait_recv()
            here = near[j, core] if n in (0, 3) else near_in[j]
            out_ref[:, columns(h)] = here + far_in[h]
    for u in range(waves):
        for n in range(3):
            far_copy(u, n).wait_send()


def on_device(n_grp, n_seq, queries, keys, values, forget, beta, level_weights):
    size = queries.shape[0]
    heads = forget.shape[1]
    dim = queries.shape[1] // heads
    slots = heads // 2
    n_mid = (n_grp * n_seq).bit_length() - 5
    dma = pltpu.SemaphoreType.DMA
    small = forget.T, beta.T, jnp.transpose(level_weights, (0, 2, 1))
    arguments = (queries, keys, values, *small)

    def vmem(*shape):
        return pltpu.VMEM(shape, F32)

    return pl.pallas_call(
        functools.partial(kernel, n_grp, n_seq, heads),
        out_shape=pltpu.VMEM((size, heads * dim), F32),
        in_specs=[pl.BlockSpec(memory_space=pl.ANY)] * 6,
        out_specs=pl.BlockSpec(memory_space=pltpu.VMEM),
        scratch_shapes=[
            vmem(heads, AUX, size),
            vmem(slots, 2 * size + AUX, dim),
            vmem(slots, size, dim),
            vmem(slots, 2 * size + AUX, dim),
            vmem(slots, size, dim),
            vmem(2, slots, size, 2 * dim),
            vmem(2, slots, size, AUX),
            vmem(2, slots, 8, size),
        ]
        + [vmem(2, slots, dim, dim)] * 2
        + [vmem(slots, dim, dim)] * 2
        + [vmem(2, 2, dim, dim)] * 2
        + [
            vmem(slots, 2, size + ROWS, dim),
            vmem(2, 2, 2, size + ROWS, dim),
            vmem(2, 2, 2, size, ROWS),
            vmem(slots, 2, size, dim),
            vmem(slots, size, dim),
            vmem(2, 2, 2, size, dim),
            vmem(heads, size, dim),
        ]
        + [vmem(n_mid, 2, 2, dim, dim)] * 2
        + [vmem(2, 4, dim, dim)] * 2
        + [pltpu.VMEM(a.shape, a.dtype) for a in arguments]
        + [dma((slots,))] * 4
        + [dma((4,))] * 4
        + [dma((n_mid, 4))] * 2
        + [dma((12,))] * 2
        + [dma((slots,))] * 2
        + [dma((6,))] * 3,
        compiler_params=pltpu.CompilerParams(collective_id=0, has_side_effects=True),
    )(*arguments)


def solution(mesh):
    both = P(("grp", "seq"), None)
    return jax.shard_map(
        functools.partial(on_device, mesh.shape["grp"], mesh.shape["seq"]),
        mesh=mesh,
        in_specs=(both, both, both, both, both, P(None, ("grp", "seq"), None)),
        out_specs=both,
        check_vma=False,
    )
```

```python
import functools

import jax
import jax.numpy as jnp
from jax import lax
from jax.experimental import pallas as pl
from jax.experimental.pallas import tpu as pltpu
from jax.sharding import PartitionSpec as P

MESH = pl.DeviceIdType.MESH
F32 = jnp.float32
BF16 = jnp.bfloat16
NN = (((1,), (0,)), ((), ()))
NT = (((1,), (1,)), ((), ()))
AUX = 16
ROWS = 8
TILE = 16
EPS = 1e-06


def dot(a, b, dims=NN):
    return lax.dot_general(a, b, dims, preferred_element_type=F32)


def split(a):
    high = a.astype(BF16)
    return high, (a - high.astype(F32)).astype(BF16)


def mm(a, b):
    ah, al = a
    bh, bl = b
    return dot(ah, bh) + (dot(ah, bl) + dot(al, bh))


def mm_square(a, b):
    ah, al = a
    bh, bl = b
    right = jnp.concatenate(
        [jnp.concatenate([bh, bl], 1), jnp.concatenate([bh, jnp.zeros_like(bl)], 1)], 0
    )
    both = dot(jnp.concatenate([ah, al], 1), right)
    width = bh.shape[1]
    return both[:, :width] + both[:, width:]


def mm_exact(a, b):
    return dot(jnp.concatenate(a, 1), jnp.concatenate([b, b], 0))


def tile_inverse(low, size):
    lane = lax.broadcasted_iota(jnp.int32, (TILE, size), 1)
    sub = lax.broadcasted_iota(jnp.int32, (TILE, size), 0)
    tile = lane // TILE
    packed = low[:TILE]
    for g in range(1, size // TILE):
        packed = jnp.where(tile == g, low[g * TILE : (g + 1) * TILE], packed)
    inner = lane - tile * TILE
    packed = jnp.where(sub > inner, packed, 0.0)
    x = jnp.where(sub == inner, 1.0, 0.0)
    for c in range(TILE - 1):
        column = jnp.take_along_axis(packed, tile * TILE + c, axis=1)
        x = x - column * x[c : c + 1]
    return jnp.concatenate(
        [jnp.where(tile == g, x, 0.0) for g in range(size // TILE)], 0
    )


def unit_lower_inverse(lowers, size, row, col):
    apart = row ^ col
    inverses = [tile_inverse(low, size) for low in lowers]
    width = TILE
    while width < size:
        mask = (apart >= width) & (apart < 2 * width)
        parts = [split(x) for x in inverses]
        blocks = [split(jnp.where(mask, low, 0.0)) for low in lowers]
        left = [split(mm_square(x, b)) for x, b in zip(parts, blocks)]
        inverses = [x - mm_square(l, p) for x, l, p in zip(inverses, left, parts)]
        width *= 2
    return inverses


def transitions(blocks, size, dim):
    row = lax.broadcasted_iota(jnp.int32, (size, size), 0)
    col = lax.broadcasted_iota(jnp.int32, (size, size), 1)
    aux_row = lax.broadcasted_iota(jnp.int32, (AUX, size), 0)
    staged, lowers = [], []
    for kb, vb, aux in blocks:
        gram = dot(kb, kb, NT)
        norm = jnp.sum(jnp.where(row == col, gram, 0.0), 0, keepdims=True) + EPS
        rk = lax.rsqrt(norm)
        gain = aux[1:2] * (rk * rk)
        decay = aux[0:1]
        cols = jnp.where(aux_row == AUX - 1, gain, aux).T
        lowers.append(jnp.where(row > col, gram * gain, 0.0))
        staged.append((kb, vb, gain, norm * rk / decay, decay[:, size - 1 : size], cols))
    inverses = unit_lower_inverse(lowers, size, row, col)
    eye = (row == col).astype(F32)
    results = []
    for inverse, (kb, vb, gain, unscale, last, cols) in zip(inverses, staged):
        y = mm_exact(split(inverse), kb)
        z = mm_exact(split(inverse * unscale), vb)
        pair = jnp.concatenate([y, z], 1)
        kt = kb.astype(F32).T.astype(BF16)
        moved = dot(
            jnp.concatenate([kt, kt], 1),
            jnp.concatenate(split(pair * cols[:, AUX - 1 : AUX]), 0),
        )
        turn, write = last * (eye - moved[:, :dim]), last * moved[:, dim:]
        results.append((turn, write, pair, cols, gain))
    return results


def local_reads(qb, kb, pair, cols, gain):
    size = qb.shape[0]
    dim = qb.shape[1]
    row = lax.broadcasted_iota(jnp.int32, (size, size), 0)
    col = lax.broadcasted_iota(jnp.int32, (size, size), 1)
    q = qb.astype(F32)
    scale = lax.rsqrt(jnp.sum(q * q, -1, keepdims=True) + EPS) * cols[:, 0:1]
    scores = jnp.where(row >= col, dot(qb, kb, NT) * gain, 0.0)
    seen = mm(split(scores), split(pair))
    return scale * (q - seen[:, :dim]), (scale * cols[:, 2:3]) * seen[:, dim:]


def chain(upper, lower):
    return mm_square(split(upper), split(lower))


def beside(turn, write):
    th, tl = split(turn)
    wh, wl = split(write)
    return jnp.concatenate([th, wh], 1), jnp.concatenate([tl, wl], 1)


def kernel(n_grp, n_seq, heads, *refs):
    arguments, out_ref = refs[:6], refs[6]
    (
        aux,
        kv_out,
        q_out,
        kv_in,
        q_in,
        pairs,
        colb,
        gains,
        turns,
        writes,
        node_t,
        node_w,
        low_t,
        low_w,
        r_out,
        r_in,
        colr,
        near,
        near_in,
        far,
        far_in,
        mid_t,
        mid_w,
        top_t,
        top_w,
        *held,
    ) = refs[7:38]
    q_ref, k_ref, v_ref, f_ref, b_ref, w_ref = held
    (
        s_kv,
        r_kv,
        s_q,
        r_q,
        s_node,
        r_node,
        s_r,
        r_r,
        s_mid,
        r_mid,
        s_top,
        r_top,
        s_near,
        r_near,
        s_far,
        r_far,
        s_load,
    ) = refs[38:]
    total_bits = (n_grp * n_seq).bit_length() - 1
    middle = list(range(2, total_bits - 2))
    xl, yl = total_bits - 2, total_bits - 1
    n_mid = len(middle)
    size = q_ref.shape[0]
    dim = q_ref.shape[1] // heads
    slots = heads // 2
    waves = slots // 2
    pos = lax.axis_index("grp") * n_seq + lax.axis_index("seq")

    def bit_of(l):
        return (pos // (1 << l)) % 2

    def where_is(number):
        return (number // n_seq, number % n_seq)

    def flipped(*ls):
        return where_is(pos + sum((1 - 2 * bit_of(l)) * (1 << l) for l in ls))

    def columns(i):
        return pl.ds(pl.multiple_of(i * dim, dim), dim)

    def remote(source, target, send, receive, device):
        return pltpu.make_async_remote_copy(
            src_ref=source,
            dst_ref=target,
            send_sem=send,
            recv_sem=receive,
            device_id=device,
            device_id_type=MESH,
        )

    core, zl, xx, yy = bit_of(0), bit_of(1), bit_of(xl), bit_of(yl)
    other = 1 - core
    beside_me, across, diagonal = flipped(0), flipped(1), flipped(0, 1)
    tops = (flipped(xl), flipped(yl), flipped(xl, yl))
    mine = 2 * yy + xx
    theirs = (2 * yy + 1 - xx, 2 * (1 - yy) + xx, 2 * (1 - yy) + 1 - xx)
    greeted = [beside_me, across, diagonal, *tops] + [flipped(l) for l in middle]
    barrier = pltpu.get_barrier_semaphore()
    for device in greeted:
        pl.semaphore_signal(barrier, inc=1, device_id=device, device_id_type=MESH)

    loads = [
        pltpu.make_async_copy(source, target, s_load.at[i])
        for i, (source, target) in enumerate(zip(arguments, held))
    ]
    for i in (3, 4, 5, 1, 2, 0):
        loads[i].start()
    for i in (3, 4, 5):
        loads[i].wait()

    total = f_ref[...]
    lane = lax.broadcasted_iota(jnp.int32, total.shape, 1)
    step = 1
    while step < size:
        total = total + jnp.where(lane >= step, pltpu.roll(total, step, 1), 0.0)
        step *= 2
    decay = jnp.exp(-total)
    aux[...] = jnp.zeros_like(aux)
    levels = w_ref.shape[0]
    for h in range(heads):
        aux[h, 0:1] = decay[h : h + 1]
        aux[h, 1:2] = b_ref[h : h + 1]
        for l in range(levels):
            aux[h, 2 + l : 3 + l] = w_ref[l, h : h + 1]

    away = [2 * u + 1 - zl for u in range(waves)]
    kept = [2 * u + zl for u in range(waves)]
    loads[1].wait()
    loads[2].wait()
    for j in away + kept:
        h = other * slots + j
        kv_out[j, :size] = k_ref[:, columns(h)].astype(F32)
        kv_out[j, size : 2 * size] = v_ref[:, columns(h)].astype(F32)
        kv_out[j, 2 * size :] = aux[h]
    pl.semaphore_wait(barrier, len(greeted))

    pending = []

    def begin(copy):
        copy.start()
        pending.append(copy)
        return copy

    def kv_copy(j):
        return remote(kv_out.at[j], kv_in.at[j], s_kv.at[j], r_kv.at[j], beside_me)

    def q_copy(j):
        return remote(q_out.at[j], q_in.at[j], s_q.at[j], r_q.at[j], beside_me)

    for j in away + kept:
        begin(kv_copy(j))

    def own_block(j):
        h = core * slots + j
        return k_ref[:, columns(h)], v_ref[:, columns(h)], aux[h]

    def other_block(j):
        return (
            kv_in[j, :size].astype(BF16),
            kv_in[j, size : 2 * size].astype(BF16),
            kv_in[j, 2 * size :],
        )

    def solve(work):
        done = transitions(
            [own_block(j) if e == 0 else other_block(j) for j, e in work], size, dim
        )
        for (j, e), (turn, write, pair, cols, gain) in zip(work, done):
            s = other if e else core
            turns[s, j] = turn
            writes[s, j] = write
            pairs[e, j] = pair
            colb[e, j] = cols
            gains[e, j] = jnp.broadcast_to(gain, (8, size))

    late = []
    node_copies = [
        [
            remote(
                source.at[2 * u + 1 - zl],
                target.at[u, zl],
                s_node.at[2 * u + n],
                r_node.at[2 * u + n],
                across,
            )
            for n, (source, target) in enumerate(((node_t, low_t), (node_w, low_w)))
        ]
        for u in range(waves)
    ]
    pending += [copy for copies in node_copies for copy in copies]

    def send_nodes(u):
        for copy in node_copies[u]:
            copy.start()

    def merge(j):
        upper = turns[1, j]
        node_t[j] = chain(upper, turns[0, j])
        node_w[j] = chain(upper, writes[0, j]) + writes[1, j]

    def send_mid(m, u, n):
        l = middle[m]
        ref = (mid_t, mid_w)[n].at[m, u, bit_of(l)]
        copy = remote(ref, ref, s_mid.at[m, 2 * u + n], r_mid.at[m, 2 * u + n], flipped(l))
        if m + 1 < n_mid:
            begin(copy)
            return
        needed = first_x | first_y | (bit_of(l) == 0)
        pl.when(needed)(copy.start)
        late.append((needed, copy))

    def wait_mid(m, u, n):
        l = middle[m]
        ref = (mid_t, mid_w)[n].at[m, u, 1 - bit_of(l)]
        remote(
            ref, ref, s_mid.at[m, 2 * u + n], r_mid.at[m, 2 * u + n], flipped(l)
        ).wait_recv()

    first_x, second_x = xx == 0, xx == 1
    first_y, second_y = yy == 0, yy == 1

    def top_copy(u, n, p, group):
        ref = (top_t, top_w)[n].at[u, group]
        i = 4 * p + 2 * u + n
        return remote(ref, ref, s_top.at[i], r_top.at[i], tops[p])

    def each_top(u, n, act):
        def do(*ps):
            def run():
                for p in ps:
                    act(top_copy(u, n, p, mine))

            return run

        if n == 1:
            pl.when(first_x)(do(0))
            pl.when(first_y)(do(1, 2))
        else:
            pl.when(first_x & second_y)(do(0))
            pl.when(second_x & first_y)(do(1, 2))

    def send_top(u, n):
        each_top(u, n, lambda copy: copy.start())

    def wait_top(u, n, p):
        top_copy(u, n, p, theirs[p]).wait_recv()

    def lift(m, u, n):
        if m < 0:
            node_copies[u][n].wait_recv()
            ts, ws = low_t.at[u], low_w.at[u]
        else:
            ts, ws = mid_t.at[m, u], mid_w.at[m, u]

        def value():
            return chain(ts[1], ts[0]) if n == 0 else chain(ts[1], ws[0]) + ws[1]

        if m + 1 < n_mid:
            if m >= 0:
                wait_mid(m, u, n)
            (mid_t, mid_w)[n][m + 1, u, bit_of(middle[m + 1])] = value()
            send_mid(m + 1, u, n)
            return

        @pl.when(first_x | first_y)
        def _():
            wait_mid(m, u, n)
            (top_t, top_w)[n][u, mine] = value()
            send_top(u, n)

        @pl.when(second_x & second_y & (bit_of(middle[m]) == 1))
        def _():
            wait_mid(m, u, n)

    def reads(group):
        for j in group:
            q_copy(j).wait_recv()
        for j in group:
            h = core * slots + j
            for e in range(2):
                if e == 0:
                    qb, kb = q_ref[:, columns(h)], k_ref[:, columns(h)]
                else:
                    qb, kb = q_in[j].astype(BF16), kv_in[j, :size].astype(BF16)
                s = other if e else core
                r, inside = local_reads(qb, kb, pairs[e, j], colb[e, j], gains[e, j, :1])
                r_out[j, s, :size] = r
                r_out[j, s, size:] = (kv_in[j, 2 * size :] if e else aux[h])[4 : 4 + ROWS]
                near[j, s] = inside
        for j in group:
            seen = mm(split(r_out[j, 1, :size]), beside(turns[0, j], writes[0, j]))
            weight = jnp.where(core == 1, colb[0, j], colb[1, j])[:, 3:4]
            r_out[j, 1, :size] = seen[:, :dim]
            near[j, 1] += weight * seen[:, dim:]

    r_copies = {}

    def send_reads(u):
        j = 2 * u + 1 - zl
        for s in range(2):
            i = 2 * u + s
            r_copies[u, s] = begin(
                remote(r_out.at[j, s], r_in.at[u, zl, s], s_r.at[i], r_r.at[i], across)
            )

    def keep_reads():
        for u in range(waves):
            for s in range(2):
                r_in[u, zl, s] = r_out[kept[u], s]

    def read(u, items, lower, l, fresh=False):
        rows = jnp.concatenate([r_in[u, z, s, :size] for z, s in items], 0)
        seen = mm(split(rows), lower)
        for n, (z, s) in enumerate(items):
            part = seen[n * size : (n + 1) * size]
            value = colr[u, z, s][:, l - 1 : l] * part[:, dim:]
            far[u, z, s] = value if fresh else far[u, z, s] + value
            r_in[u, z, s, :size] = part[:, :dim]

    everyone = [(z, s) for z in range(2) for s in range(2)]

    def low_reads(u):
        for s in range(2):
            r_copies[u, s].wait_recv()
        for z, s in everyone:
            colr[u, z, s] = r_in[u, z, s, size:].T
        for s in range(2):
            far[u, 0, s] = jnp.zeros((size, dim), F32)
        read(u, everyone[2:], beside(low_t[u, 0], low_w[u, 0]), 1, fresh=True)

    def mid_reads(u):
        for m, l in enumerate(middle):

            @pl.when(bit_of(l) == 1)
            def _():
                read(u, everyone, beside(mid_t[m, u, 0], mid_w[m, u, 0]), l)

    def far_copy(u, n):
        z, s, device = (
            (1 - zl, core, across),
            (1 - zl, other, diagonal),
            (zl, other, beside_me),
        )[n]
        h = core * slots + 2 * u + zl
        i = 3 * u + n
        return remote(far.at[u, z, s], far_in.at[h], s_far.at[i], r_far.at[i], device)

    def top_reads(u):
        @pl.when(second_x)
        def _():
            wait_top(u, 1, 0)
            pl.when(second_y)(functools.partial(wait_top, u, 0, 0))
            read(u, everyone, beside(top_t[u, 2 * yy], top_w[u, 2 * yy]), xl)

        @pl.when(second_y)
        def _():
            pl.when(second_x)(functools.partial(wait_top, u, 0, 1))
            pl.when(first_x)(functools.partial(wait_top, u, 0, 2))
            wait_top(u, 1, 1)
            wait_top(u, 1, 2)
            lower = split(chain(top_t[u, 1], top_w[u, 0]) + top_w[u, 1])
            for n, (z, s) in enumerate(
                ((1 - zl, core), (1 - zl, other), (zl, other), (zl, core))
            ):
                seen = mm(split(r_in[u, z, s, :size]), lower)
                far[u, z, s] += colr[u, z, s][:, yl - 1 : yl] * seen
                if n < 3:
                    far_copy(u, n).start()

        @pl.when(first_y)
        def _():
            for n in range(3):
                far_copy(u, n).start()

        far_in[core * slots + 2 * u + zl] = far[u, zl, core]

    solve([(j, 0) for j in away])
    loads[0].wait()
    for j in range(slots):
        q_out[j] = q_ref[:, columns(other * slots + j)].astype(F32)
    for j in range(slots):
        begin(q_copy(j))
    for j in away:
        kv_copy(j).wait_recv()
    solve([(j, 1) for j in away])
    for u in range(waves):
        merge(away[u])
    for n in range(2):
        node_copies[0][n].start()
    for n in range(2):
        node_copies[1][n].start()
    for j in kept:
        kv_copy(j).wait_recv()
    solve([(j, e) for j in kept for e in range(2)])
    for u in range(waves):
        merge(kept[u])
        low_t[u, zl] = node_t[kept[u]]
        low_w[u, zl] = node_w[kept[u]]
    lift(-1, 0, 0)
    lift(-1, 0, 1)
    reads(away[:1])
    send_reads(0)
    reads(away[1:])
    for m in range(n_mid - 1):
        lift(m, 0, 0)
        lift(m, 0, 1)
    lift(n_mid - 1, 0, 0)
    lift(-1, 1, 0)
    lift(-1, 1, 1)
    send_reads(1)
    reads(kept)
    keep_reads()
    near_copies = [
        begin(
            remote(near.at[j, other], near_in.at[j], s_near.at[j], r_near.at[j], beside_me)
        )
        for j in range(slots)
    ]
    lift(n_mid - 1, 0, 1)
    for m in range(n_mid - 1):
        lift(m, 1, 0)
        lift(m, 1, 1)
    lift(n_mid - 1, 1, 0)
    lift(n_mid - 1, 1, 1)
    for u in range(waves):
        low_reads(u)
        mid_reads(u)
        top_reads(u)

    for u in range(waves):
        for n in range(2):
            each_top(u, n, lambda copy: copy.wait_send())
    for copy in pending:
        copy.wait_send()
    for needed, copy in late:
        pl.when(needed)(copy.wait_send)
    for copy in near_copies:
        copy.wait_recv()
    for u in range(waves):
        for n, (c, z) in enumerate(((core, 1 - zl), (other, 1 - zl), (other, zl), (core, zl))):
            j = 2 * u + z
            h = c * slots + j
            if n < 3:
                i = 3 * u + n
                device = (across, diagonal, beside_me)[n]
                remote(
                    far.at[u, zl, core], far_in.at[h], s_far.at[i], r_far.at[i], device
                ).wait_recv()
            here = near[j, core] if n in (0, 3) else near_in[j]
            out_ref[:, columns(h)] = here + far_in[h]
    for u in range(waves):
        for n in range(3):
            far_copy(u, n).wait_send()


def on_device(n_grp, n_seq, queries, keys, values, forget, beta, level_weights):
    size = queries.shape[0]
    heads = forget.shape[1]
    dim = queries.shape[1] // heads
    slots = heads // 2
    n_mid = (n_grp * n_seq).bit_length() - 5
    dma = pltpu.SemaphoreType.DMA
    small = forget.T, beta.T, jnp.transpose(level_weights, (0, 2, 1))
    arguments = (queries, keys, values, *small)

    def vmem(*shape):
        return pltpu.VMEM(shape, F32)

    return pl.pallas_call(
        functools.partial(kernel, n_grp, n_seq, heads),
        out_shape=pltpu.VMEM((size, heads * dim), F32),
        in_specs=[pl.BlockSpec(memory_space=pl.ANY)] * 6,
        out_specs=pl.BlockSpec(memory_space=pltpu.VMEM),
        scratch_shapes=[
            vmem(heads, AUX, size),
            vmem(slots, 2 * size + AUX, dim),
            vmem(slots, size, dim),
            vmem(slots, 2 * size + AUX, dim),
            vmem(slots, size, dim),
            vmem(2, slots, size, 2 * dim),
            vmem(2, slots, size, AUX),
            vmem(2, slots, 8, size),
        ]
        + [vmem(2, slots, dim, dim)] * 2
        + [vmem(slots, dim, dim)] * 2
        + [vmem(2, 2, dim, dim)] * 2
        + [
            vmem(slots, 2, size + ROWS, dim),
            vmem(2, 2, 2, size + ROWS, dim),
            vmem(2, 2, 2, size, ROWS),
            vmem(slots, 2, size, dim),
            vmem(slots, size, dim),
            vmem(2, 2, 2, size, dim),
            vmem(heads, size, dim),
        ]
        + [vmem(n_mid, 2, 2, dim, dim)] * 2
        + [vmem(2, 4, dim, dim)] * 2
        + [pltpu.VMEM(a.shape, a.dtype) for a in arguments]
        + [dma((slots,))] * 4
        + [dma((4,))] * 4
        + [dma((n_mid, 4))] * 2
        + [dma((12,))] * 2
        + [dma((slots,))] * 2
        + [dma((6,))] * 3,
        compiler_params=pltpu.CompilerParams(
            collective_id=0,
            has_side_effects=True,
        ),
    )(*arguments)


def solution(mesh):
    both = P(("grp", "seq"), None)
    return jax.shard_map(
        functools.partial(on_device, mesh.shape["grp"], mesh.shape["seq"]),
        mesh=mesh,
        in_specs=(both, both, both, both, both, P(None, ("grp", "seq"), None)),
        out_specs=both,
        check_vma=False,
    )
```
